128 devices in a mesh: row: 16 (over z_hi, y, core), col: 8 (over z_lo, x).
Axes of the slice: x: 4, y: 4, z: 4 (z_hi: 2, z_lo: 2; z = z_hi * 2 + z_lo), core: 2. Of those that a mesh axis runs over, the one named last changes fastest.
Arguments:
- multispectral: bfloat16 [2, 32768, 4096], P(None, 'row', 'col'), may hold values from -6 to 6
- hyperspectral: bfloat16 [96, 8192, 1024], P(None, 'row', 'col'), may hold values from -6 to 6
- row_start: float32 [32768, 128], P(('row', 'col')), may hold values from -6 to 6
- col_factor: bfloat16 [4096, 128], P('col', 'row'), may hold values from -0.09375 to 0.09375
- band_factor: float32 [96, 128], replicated, may hold values from -2 to 2
- response: float32 [2, 96], replicated, may hold values from 0.2 to 1
- blur_taps: float32 [9], replicated, may hold values from 0.2 to 1
- offsets: int32 [9], replicated, may hold values from -8 to 8, as said below
Outputs:
- row_factor: float32 [32768, 128], P(('row', 'col'))
- residual: float32 [32768, 128], P(('row', 'col'))
The draws below stay inside these ranges and needn't reach their ends.
Inputs may be any that keep to these rules, and one draw needn't show every extreme that they name: 9 distinct offsets; -8 and 8 are always among them.
All inputs are finite; a program needn't handle non-finite values.
Results may differ from the reference program's by a relative error of at most 0.0023.
Values may be sent and summed in bfloat16 or wider, within the bound.
A program may use at most 128 MiB of HBM per device.

```python
import math
import jax
import jax.numpy as jnp
from jax import lax

R = 128
KH = 96
KM = 2
DEC = 4
W = 8
TAPS = 9
ITERS = 4
NI = 32768
NJ = 4096
IH = 8192
JH = 1024


def draw_offsets(key, part):
    middle = jnp.arange(1, 2 * W, dtype=jnp.int32) - W
    picked = jax.random.permutation(key, middle)[:TAPS - 2]
    ends = jnp.array([-W, W], dtype=jnp.int32)
    return jnp.concatenate([ends, picked]).astype(jnp.int32)


def level_of(own_key, dims, shards, smallest, top_value):
    level = 1.0
    for dim, shards_of in shards:
        draws = jax.random.uniform(jax.random.fold_in(jax.random.fold_in(own_key, 6), dim), (shards_of,), jnp.float32, smallest / len(shards), top_value / len(shards))
        level = level * jnp.repeat(jnp.exp(draws), dims[dim] // shards_of).reshape((-1,) + (1,) * (len(dims) - 1 - dim))
    return level


def centred(stream_key, extent, width, most, pieces=(), kind=jnp.bfloat16):
    drawn = width * jax.random.normal(stream_key, extent, jnp.float32)
    if pieces:
        drawn = drawn * level_of(stream_key, extent, pieces, -0.22, 0.18)
    return jnp.clip(drawn, -most, most).astype(kind)


def setup_inputs(seed: int = 0) -> dict:
    streams_of = jax.random.split(jax.random.key(seed), 9)
    return {
        "multispectral": centred(streams_of[0], (KM, NI, NJ), 1.0, 6.0, ((1, 16), (2, 8))),
        "hyperspectral": centred(streams_of[1], (KH, IH, JH), 1.0, 6.0, ((1, 16), (2, 8))),
        "row_start": centred(streams_of[2], (NI, R), 1.0, 6.0, ((0, 128),), jnp.float32),
        "col_factor": centred(streams_of[3], (NJ, R), NJ ** -0.5, 0.09375, ((0, 8), (1, 16))),
        "band_factor": centred(streams_of[4], (KH, R), 0.15, 2.0, (), jnp.float32),
        "response": jnp.clip(jax.random.uniform(streams_of[5], (KM, KH), jnp.float32, 0.2, 1.0), 0.2, 1.0),
        "blur_taps": jnp.clip(jnp.exp(jax.random.uniform(streams_of[6], (TAPS,), jnp.float32, math.log(0.2), math.log(1.0))), 0.2, 1.0),
        "offsets": draw_offsets(jax.random.fold_in(streams_of[8], 71), 0),
    }


RIDGE_TERM = 0.1
FULL_PRECISION = lax.Precision.HIGHEST


def blur_down(values, weights, offsets):
    height = values.shape[0]
    result = jnp.zeros((height // DEC, values.shape[1]), jnp.float32)
    for number in range(TAPS):
        shifted = jnp.roll(values, -offsets[number], axis=0)
        picked = shifted.reshape(height // DEC, DEC, values.shape[1])[:, 0, :]
        result = result + weights[number] * picked.astype(jnp.float32)
    return result


def blur_up(coarse, weights, offsets):
    height, columns = coarse.shape
    padding = jnp.zeros((height, DEC - 1, columns), jnp.float32)
    spread_rows = jnp.concatenate([coarse[:, None, :], padding], axis=1).reshape(height * DEC, columns)
    result = jnp.zeros((height * DEC, columns), jnp.float32)
    for number in range(TAPS):
        result = result + weights[number] * jnp.roll(spread_rows, offsets[number], axis=0)
    return result


def reference(multispectral, hyperspectral, row_start, col_factor, band_factor, response, blur_taps, offsets):
    coarse_columns = blur_down(col_factor, blur_taps, offsets)
    merged = jnp.dot(response, band_factor, precision=FULL_PRECISION)
    multi_pairs = (merged[:, None, :] * col_factor.astype(jnp.float32)[None, :, :]).astype(jnp.bfloat16)
    hyper_pairs = (band_factor[:, None, :] * coarse_columns[None, :, :]).astype(jnp.bfloat16)
    multi_sums = jnp.zeros((NI, R), jnp.float32)
    for channel in range(KM):
        multi_sums = multi_sums + jnp.dot(multispectral[channel], multi_pairs[channel], preferred_element_type=jnp.float32)
    hyper_sums = jnp.zeros((IH, R), jnp.float32)
    for channel in range(KH):
        hyper_sums = hyper_sums + jnp.dot(hyperspectral[channel], hyper_pairs[channel], preferred_element_type=jnp.float32)
    column_gram = jnp.dot(col_factor.T, col_factor, preferred_element_type=jnp.float32)
    coarse_gram = jnp.dot(coarse_columns.T, coarse_columns, precision=FULL_PRECISION)
    band_gram = jnp.dot(band_factor.T, band_factor, precision=FULL_PRECISION)
    merged_gram = jnp.dot(merged.T, merged, precision=FULL_PRECISION)
    hyper_gram = coarse_gram * band_gram
    multi_gram = column_gram * merged_gram

    def operate(values):
        restored = blur_up(blur_down(values, blur_taps, offsets), blur_taps, offsets)
        return (jnp.dot(restored, hyper_gram, precision=FULL_PRECISION)
                + jnp.dot(values, multi_gram, precision=FULL_PRECISION) + RIDGE_TERM * values)

    right_side = blur_up(hyper_sums, blur_taps, offsets) + multi_sums
    solution = row_start
    residual = right_side - operate(solution)
    direction = residual
    norm_now = jnp.sum(residual * residual)
    for iteration in range(ITERS):
        mapped = operate(direction)
        step_size = norm_now / jnp.sum(direction * mapped)
        solution = solution + step_size * direction
        residual = residual - step_size * mapped
        norm_next = jnp.sum(residual * residual)
        direction = residual + (norm_next / norm_now) * direction
        norm_now = norm_next
    return solution, residual
```

```python
import jax
import jax.numpy as jnp
from jax import lax
from jax.sharding import PartitionSpec as P

DEC = 4
W = 8
ITERS = 4


RIDGE_TERM = 0.1
FULL_PRECISION = lax.Precision.HIGHEST


def extended(cells, sides, width):
    for axis, dim in sides:
        count = lax.axis_size(axis)
        head = lax.slice_in_dim(cells, 0, width, axis=dim)
        tail = lax.slice_in_dim(cells, cells.shape[dim] - width, cells.shape[dim], axis=dim)
        cells = jnp.concatenate(
            [
                lax.ppermute(tail, axis, [(i, (i + 1) % count) for i in range(count)]),
                cells,
                lax.ppermute(head, axis, [((i + 1) % count, i) for i in range(count)]),
            ],
            axis=dim,
        )
    return cells


def tap_places(offsets):
    reach = offsets + W
    return reach // DEC, reach % DEC


def blur_down(wide, weights, offsets, rows_out):
    shifts, phases = tap_places(offsets)
    quads = wide.reshape(wide.shape[0] // DEC, DEC, wide.shape[1])
    total = jnp.zeros((rows_out, wide.shape[1]), jnp.float32)
    for number in range(weights.shape[0]):
        piece = lax.dynamic_slice(
            quads, (shifts[number], phases[number], 0), (rows_out, 1, wide.shape[1])
        )[:, 0, :]
        total = total + weights[number] * piece.astype(jnp.float32)
    return total


def blur_up(coarse_wide, weights, offsets, margin):
    shifts, phases = tap_places(offsets)
    rows = coarse_wide.shape[0] - 2 * margin
    columns = coarse_wide.shape[1]
    parts = [jnp.zeros((rows, columns), jnp.float32) for _ in range(DEC)]
    for number in range(weights.shape[0]):
        piece = lax.dynamic_slice_in_dim(coarse_wide, margin + 2 - shifts[number], rows, 0)
        for phase in range(DEC):
            scale = jnp.where(phases[number] == phase, weights[number], jnp.float32(0.0))
            parts[phase] = parts[phase] + scale * piece
    return jnp.stack(parts, axis=1).reshape(rows * DEC, columns)


def body(
    multispectral, hyperspectral, row_start, col_factor, band_factor, response, blur_taps, offsets
):
    low_reach = (W + DEC - 1) // DEC
    columns = lax.all_gather(col_factor, "row", axis=1, tiled=True)
    column_wide = extended(columns, (("col", 0),), W)
    coarse_columns = blur_down(column_wide, blur_taps, offsets, columns.shape[0] // DEC)
    merged = jnp.dot(response, band_factor, precision=FULL_PRECISION)
    multi_pairs = (merged[:, None, :] * columns.astype(jnp.float32)[None, :, :]).astype(
        jnp.bfloat16
    )
    hyper_pairs = (band_factor[:, None, :] * coarse_columns[None, :, :]).astype(jnp.bfloat16)
    multi_part = jnp.einsum(
        "kij,kjr->ir", multispectral, multi_pairs, preferred_element_type=jnp.float32
    )
    hyper_part = jnp.einsum(
        "kij,kjr->ir", hyperspectral, hyper_pairs, preferred_element_type=jnp.float32
    )
    column_part = jnp.einsum("jr,js->rs", columns, columns, preferred_element_type=jnp.float32)
    coarse_part = jnp.einsum("jr,js->rs", coarse_columns, coarse_columns, precision=FULL_PRECISION)
    column_gram, coarse_gram = lax.psum((column_part, coarse_part), "col")
    band_gram = jnp.dot(band_factor.T, band_factor, precision=FULL_PRECISION)
    merged_gram = jnp.dot(merged.T, merged, precision=FULL_PRECISION)
    hyper_gram = coarse_gram * band_gram
    multi_gram = column_gram * merged_gram
    multi_sums, hyper_sums = lax.psum((multi_part, hyper_part), "col")
    start_rows = lax.all_gather(row_start, "col", axis=0, tiled=True)

    def inner_sum(first_field, second_field):
        return lax.psum(jnp.sum(first_field * second_field), "row")

    fine_rows = start_rows.shape[0]
    coarse_rows = fine_rows // DEC
    fine_reach = W + DEC * low_reach

    def operate(values):
        fine_wide = extended(values, (("row", 0),), fine_reach)
        coarse_wide = blur_down(fine_wide, blur_taps, offsets, coarse_rows + 2 * low_reach)
        restored = blur_up(coarse_wide, blur_taps, offsets, low_reach)
        return (
            jnp.dot(restored, hyper_gram, precision=FULL_PRECISION)
            + jnp.dot(values, multi_gram, precision=FULL_PRECISION)
            + RIDGE_TERM * values
        )

    hyper_wide = extended(hyper_sums, (("row", 0),), low_reach)
    right_side = blur_up(hyper_wide, blur_taps, offsets, low_reach) + multi_sums
    solution = start_rows
    residual = right_side - operate(solution)
    direction = residual
    norm_now = inner_sum(residual, residual)
    for iteration in range(ITERS):
        mapped = operate(direction)
        step_size = norm_now / inner_sum(direction, mapped)
        solution = solution + step_size * direction
        residual = residual - step_size * mapped
        norm_next = inner_sum(residual, residual)
        direction = residual + norm_next / norm_now * direction
        norm_now = norm_next
    portion = solution.shape[0] // lax.axis_size("col")
    corner = lax.axis_index("col") * portion
    solution = lax.dynamic_slice_in_dim(solution, corner, portion, 0)
    residual = lax.dynamic_slice_in_dim(residual, corner, portion, 0)
    return (solution, residual)


def solution(mesh):
    in_specs = (
        P(None, "row", "col"),
        P(None, "row", "col"),
        P(("row", "col"), None),
        P("col", "row"),
        P(),
        P(),
        P(),
        P(),
    )
    out_specs = (P(("row", "col"), None), P(("row", "col"), None))
    return jax.shard_map(body, mesh=mesh, in_specs=in_specs, out_specs=out_specs, check_vma=False)
```

```python
import functools

import jax
import jax.numpy as jnp
from jax import lax
from jax.experimental import pallas as pl
from jax.experimental.pallas import tpu as pltpu
from jax.sharding import PartitionSpec as P

MESH = pl.DeviceIdType.MESH

DEC = 4
W = 8
ITERS = 4


RIDGE_TERM = 0.1
FULL_PRECISION = lax.Precision.HIGHEST


def extended(cells, sides, width):
    for axis, dim in sides:
        count = lax.axis_size(axis)
        head = lax.slice_in_dim(cells, 0, width, axis=dim)
        tail = lax.slice_in_dim(cells, cells.shape[dim] - width, cells.shape[dim], axis=dim)
        cells = jnp.concatenate(
            [
                lax.ppermute(tail, axis, [(i, (i + 1) % count) for i in range(count)]),
                cells,
                lax.ppermute(head, axis, [((i + 1) % count, i) for i in range(count)]),
            ],
            axis=dim,
        )
    return cells


def tap_places(offsets):
    reach = offsets + W
    return reach // DEC, reach % DEC


def blur_down(wide, weights, offsets, rows_out):
    shifts, phases = tap_places(offsets)
    quads = wide.reshape(wide.shape[0] // DEC, DEC, wide.shape[1])
    total = jnp.zeros((rows_out, wide.shape[1]), jnp.float32)
    for number in range(weights.shape[0]):
        piece = lax.dynamic_slice(
            quads, (shifts[number], phases[number], 0), (rows_out, 1, wide.shape[1])
        )[:, 0, :]
        total = total + weights[number] * piece.astype(jnp.float32)
    return total


def blur_up(coarse_wide, weights, offsets, margin):
    shifts, phases = tap_places(offsets)
    rows = coarse_wide.shape[0] - 2 * margin
    columns = coarse_wide.shape[1]
    parts = [jnp.zeros((rows, columns), jnp.float32) for _ in range(DEC)]
    for number in range(weights.shape[0]):
        piece = lax.dynamic_slice_in_dim(coarse_wide, margin + 2 - shifts[number], rows, 0)
        for phase in range(DEC):
            scale = jnp.where(phases[number] == phase, weights[number], jnp.float32(0.0))
            parts[phase] = parts[phase] + scale * piece
    return jnp.stack(parts, axis=1).reshape(rows * DEC, columns)


def total_kernel(count, part_ref, out_ref, held, send_sems, recv_sems):
    me = lax.axis_index("row")
    col = lax.axis_index("col")
    barrier = pltpu.get_barrier_semaphore()
    for shift in range(1, count):
        pl.semaphore_signal(
            barrier, inc=1, device_id=(lax.rem(me + shift, count), col), device_id_type=MESH
        )
    pl.semaphore_wait(barrier, count - 1)
    copies = []
    for shift in range(1, count):
        copy = pltpu.make_async_remote_copy(
            src_ref=part_ref,
            dst_ref=held.at[me],
            send_sem=send_sems.at[shift],
            recv_sem=recv_sems.at[shift],
            device_id=(lax.rem(me + shift, count), col),
            device_id_type=MESH,
        )
        copy.start()
        copies.append(copy)
    held[me] = part_ref[...]
    for copy in copies:
        copy.wait()
    total = held[0]
    for source in range(1, count):
        total = total + held[source]
    out_ref[...] = total


def row_totals(parts):
    count = lax.axis_size("row")
    lanes = jnp.pad(jnp.stack(parts), (0, 128 - len(parts)))
    tile = jnp.broadcast_to(lanes[None, :], (8, 128))
    summed = pl.pallas_call(
        functools.partial(total_kernel, count),
        out_shape=jax.ShapeDtypeStruct((8, 128), jnp.float32),
        in_specs=[pl.BlockSpec(memory_space=pltpu.VMEM)],
        out_specs=pl.BlockSpec(memory_space=pltpu.VMEM),
        scratch_shapes=[
            pltpu.VMEM((count, 8, 128), jnp.float32),
            pltpu.SemaphoreType.DMA((count,)),
            pltpu.SemaphoreType.DMA((count,)),
        ],
        compiler_params=pltpu.CompilerParams(collective_id=0, has_side_effects=True),
    )(tile)
    return [summed[0, number] for number in range(len(parts))]


def body(
    multispectral, hyperspectral, row_start, col_factor, band_factor, response, blur_taps, offsets
):
    low_reach = (W + DEC - 1) // DEC
    columns = lax.all_gather(col_factor, "row", axis=1, tiled=True)
    column_wide = extended(columns, (("col", 0),), W)
    coarse_columns = blur_down(column_wide, blur_taps, offsets, columns.shape[0] // DEC)
    merged = jnp.dot(response, band_factor, precision=FULL_PRECISION)
    multi_pairs = (merged[:, None, :] * columns.astype(jnp.float32)[None, :, :]).astype(
        jnp.bfloat16
    )
    hyper_pairs = (band_factor[:, None, :] * coarse_columns[None, :, :]).astype(jnp.bfloat16)
    multi_part = jnp.einsum(
        "kij,kjr->ir", multispectral, multi_pairs, preferred_element_type=jnp.float32
    )
    hyper_part = jnp.einsum(
        "kij,kjr->ir", hyperspectral, hyper_pairs, preferred_element_type=jnp.float32
    )
    column_part = jnp.einsum("jr,js->rs", columns, columns, preferred_element_type=jnp.float32)
    coarse_part = jnp.einsum("jr,js->rs", coarse_columns, coarse_columns, precision=FULL_PRECISION)
    column_gram, coarse_gram = lax.psum((column_part, coarse_part), "col")
    band_gram = jnp.dot(band_factor.T, band_factor, precision=FULL_PRECISION)
    merged_gram = jnp.dot(merged.T, merged, precision=FULL_PRECISION)
    hyper_gram = coarse_gram * band_gram
    multi_gram = column_gram * merged_gram
    multi_sums, hyper_sums = lax.psum((multi_part, hyper_part), "col")
    start_rows = lax.all_gather(row_start, "col", axis=0, tiled=True)

    def inner_sum(first_field, second_field):
        return row_totals([jnp.sum(first_field * second_field)])[0]

    fine_rows = start_rows.shape[0]
    coarse_rows = fine_rows // DEC
    fine_reach = W + DEC * low_reach

    def operate(values):
        fine_wide = extended(values, (("row", 0),), fine_reach)
        coarse_wide = blur_down(fine_wide, blur_taps, offsets, coarse_rows + 2 * low_reach)
        restored = blur_up(coarse_wide, blur_taps, offsets, low_reach)
        return (
            jnp.dot(restored, hyper_gram, precision=FULL_PRECISION)
            + jnp.dot(values, multi_gram, precision=FULL_PRECISION)
            + RIDGE_TERM * values
        )

    hyper_wide = extended(hyper_sums, (("row", 0),), low_reach)
    right_side = blur_up(hyper_wide, blur_taps, offsets, low_reach) + multi_sums
    solution = start_rows
    residual = right_side - operate(solution)
    direction = residual
    norm_now = None
    for iteration in range(ITERS):
        mapped = operate(direction)
        if norm_now is None:
            norm_now, curvature = row_totals(
                [jnp.sum(residual * residual), jnp.sum(direction * mapped)]
            )
        else:
            curvature = inner_sum(direction, mapped)
        step_size = norm_now / curvature
        solution = solution + step_size * direction
        residual = residual - step_size * mapped
        norm_next = inner_sum(residual, residual)
        direction = residual + norm_next / norm_now * direction
        norm_now = norm_next
    portion = solution.shape[0] // lax.axis_size("col")
    corner = lax.axis_index("col") * portion
    solution = lax.dynamic_slice_in_dim(solution, corner, portion, 0)
    residual = lax.dynamic_slice_in_dim(residual, corner, portion, 0)
    return (solution, residual)


def solution(mesh):
    in_specs = (
        P(None, "row", "col"),
        P(None, "row", "col"),
        P(("row", "col"), None),
        P("col", "row"),
        P(),
        P(),
        P(),
        P(),
    )
    out_specs = (P(("row", "col"), None), P(("row", "col"), None))
    return jax.shard_map(body, mesh=mesh, in_specs=in_specs, out_specs=out_specs, check_vma=False)
```

```python
import functools

import jax
import jax.numpy as jnp
from jax import lax
from jax.experimental import pallas as pl
from jax.experimental.pallas import tpu as pltpu
from jax.sharding import PartitionSpec as P

MESH = pl.DeviceIdType.MESH

DEC = 4
W = 8
ITERS = 4


RIDGE_TERM = 0.1
FULL_PRECISION = lax.Precision.HIGHEST


def extended(cells, sides, width):
    for axis, dim in sides:
        names = axis if isinstance(axis, tuple) else (axis,)
        count = 1
        for name in names:
            count *= lax.axis_size(name)
        head = lax.slice_in_dim(cells, 0, width, axis=dim)
        tail = lax.slice_in_dim(cells, cells.shape[dim] - width, cells.shape[dim], axis=dim)
        cells = jnp.concatenate(
            [
                lax.ppermute(tail, axis, [(i, (i + 1) % count) for i in range(count)]),
                cells,
                lax.ppermute(head, axis, [((i + 1) % count, i) for i in range(count)]),
            ],
            axis=dim,
        )
    return cells


def tap_places(offsets):
    reach = offsets + W
    return reach // DEC, reach % DEC


def blur_down(wide, weights, offsets, rows_out):
    shifts, phases = tap_places(offsets)
    quads = wide.reshape(wide.shape[0] // DEC, DEC, wide.shape[1])
    total = jnp.zeros((rows_out, wide.shape[1]), jnp.float32)
    for number in range(weights.shape[0]):
        piece = lax.dynamic_slice(
            quads, (shifts[number], phases[number], 0), (rows_out, 1, wide.shape[1])
        )[:, 0, :]
        total = total + weights[number] * piece.astype(jnp.float32)
    return total


def blur_up(coarse_wide, weights, offsets, margin):
    shifts, phases = tap_places(offsets)
    rows = coarse_wide.shape[0] - 2 * margin
    columns = coarse_wide.shape[1]
    parts = [jnp.zeros((rows, columns), jnp.float32) for _ in range(DEC)]
    for number in range(weights.shape[0]):
        piece = lax.dynamic_slice_in_dim(coarse_wide, margin + 2 - shifts[number], rows, 0)
        for phase in range(DEC):
            scale = jnp.where(phases[number] == phase, weights[number], jnp.float32(0.0))
            parts[phase] = parts[phase] + scale * piece
    return jnp.stack(parts, axis=1).reshape(rows * DEC, columns)


def total_kernel(rows, cols, part_ref, out_ref, col_held, row_held, sends, receipts):
    here_row = lax.axis_index("row")
    here_col = lax.axis_index("col")
    col_peers = [(here_row, lax.rem(here_col + shift, cols)) for shift in range(1, cols)]
    row_peers = [(lax.rem(here_row + shift, rows), here_col) for shift in range(1, rows)]
    barrier = pltpu.get_barrier_semaphore()
    for peer in col_peers + row_peers:
        pl.semaphore_signal(barrier, inc=1, device_id=peer, device_id_type=MESH)
    pl.semaphore_wait(barrier, len(col_peers) + len(row_peers))
    copies = []
    for number, peer in enumerate(col_peers):
        copy = pltpu.make_async_remote_copy(
            src_ref=part_ref,
            dst_ref=col_held.at[here_col],
            send_sem=sends.at[number],
            recv_sem=receipts.at[number],
            device_id=peer,
            device_id_type=MESH,
        )
        copy.start()
        copies.append(copy)
    col_held[here_col] = part_ref[...]
    for copy in copies:
        copy.wait()
    col_total = col_held[0]
    for source in range(1, cols):
        col_total = col_total + col_held[source]
    row_held[here_row] = col_total
    copies = []
    for number, peer in enumerate(row_peers):
        copy = pltpu.make_async_remote_copy(
            src_ref=row_held.at[here_row],
            dst_ref=row_held.at[here_row],
            send_sem=sends.at[cols + number],
            recv_sem=receipts.at[cols + number],
            device_id=peer,
            device_id_type=MESH,
        )
        copy.start()
        copies.append(copy)
    for copy in copies:
        copy.wait()
    total = row_held[0]
    for source in range(1, rows):
        total = total + row_held[source]
    out_ref[...] = total


def grid_totals(parts):
    rows = lax.axis_size("row")
    cols = lax.axis_size("col")
    lanes = jnp.pad(jnp.stack(parts), (0, 128 - len(parts)))
    tile = jnp.broadcast_to(lanes[None, :], (8, 128))
    summed = pl.pallas_call(
        functools.partial(total_kernel, rows, cols),
        out_shape=jax.ShapeDtypeStruct((8, 128), jnp.float32),
        in_specs=[pl.BlockSpec(memory_space=pltpu.VMEM)],
        out_specs=pl.BlockSpec(memory_space=pltpu.VMEM),
        scratch_shapes=[
            pltpu.VMEM((cols, 8, 128), jnp.float32),
            pltpu.VMEM((rows, 8, 128), jnp.float32),
            pltpu.SemaphoreType.DMA((rows + cols,)),
            pltpu.SemaphoreType.DMA((rows + cols,)),
        ],
        compiler_params=pltpu.CompilerParams(collective_id=0, has_side_effects=True),
    )(tile)
    return [summed[0, number] for number in range(len(parts))]


def body(
    multispectral, hyperspectral, row_start, col_factor, band_factor, response, blur_taps, offsets
):
    low_reach = (W + DEC - 1) // DEC
    columns = lax.all_gather(col_factor, "row", axis=1, tiled=True)
    column_wide = extended(columns, (("col", 0),), W)
    coarse_columns = blur_down(column_wide, blur_taps, offsets, columns.shape[0] // DEC)
    merged = jnp.dot(response, band_factor, precision=FULL_PRECISION)
    multi_pairs = (merged[:, None, :] * columns.astype(jnp.float32)[None, :, :]).astype(
        jnp.bfloat16
    )
    hyper_pairs = (band_factor[:, None, :] * coarse_columns[None, :, :]).astype(jnp.bfloat16)
    multi_part = jnp.einsum(
        "kij,kjr->ir", multispectral, multi_pairs, preferred_element_type=jnp.float32
    )
    hyper_part = jnp.einsum(
        "kij,kjr->ir", hyperspectral, hyper_pairs, preferred_element_type=jnp.float32
    )
    column_part = jnp.einsum("jr,js->rs", columns, columns, preferred_element_type=jnp.float32)
    coarse_part = jnp.einsum("jr,js->rs", coarse_columns, coarse_columns, precision=FULL_PRECISION)
    column_gram, coarse_gram = lax.psum((column_part, coarse_part), "col")
    band_gram = jnp.dot(band_factor.T, band_factor, precision=FULL_PRECISION)
    merged_gram = jnp.dot(merged.T, merged, precision=FULL_PRECISION)
    hyper_gram = coarse_gram * band_gram
    multi_gram = column_gram * merged_gram
    cols = lax.axis_size("col")
    multi_blocks = multi_part.reshape(cols, -1, multi_part.shape[1])
    hyper_blocks = hyper_part.reshape(cols, -1, hyper_part.shape[1])
    joined = jnp.concatenate([multi_blocks, hyper_blocks], axis=1)
    joined = lax.psum_scatter(
        joined.reshape(-1, joined.shape[2]), "col", scatter_dimension=0, tiled=True
    )
    multi_sums = joined[: multi_blocks.shape[1]]
    hyper_sums = joined[multi_blocks.shape[1] :]
    start_rows = row_start
    grid = ("row", "col")

    def inner_sum(first_field, second_field):
        return grid_totals([jnp.sum(first_field * second_field)])[0]

    fine_rows = start_rows.shape[0]
    coarse_rows = fine_rows // DEC
    fine_reach = W + DEC * low_reach

    def operate(values):
        fine_wide = extended(values, ((grid, 0),), fine_reach)
        coarse_wide = blur_down(fine_wide, blur_taps, offsets, coarse_rows + 2 * low_reach)
        restored = blur_up(coarse_wide, blur_taps, offsets, low_reach)
        return (
            jnp.dot(restored, hyper_gram, precision=FULL_PRECISION)
            + jnp.dot(values, multi_gram, precision=FULL_PRECISION)
            + RIDGE_TERM * values
        )

    hyper_wide = extended(hyper_sums, ((grid, 0),), low_reach)
    right_side = blur_up(hyper_wide, blur_taps, offsets, low_reach) + multi_sums
    solution = start_rows
    residual = right_side - operate(solution)
    direction = residual
    norm_now = None
    for iteration in range(ITERS):
        mapped = operate(direction)
        if norm_now is None:
            norm_now, curvature = grid_totals(
                [jnp.sum(residual * residual), jnp.sum(direction * mapped)]
            )
        else:
            curvature = inner_sum(direction, mapped)
        step_size = norm_now / curvature
        solution = solution + step_size * direction
        residual = residual - step_size * mapped
        norm_next = inner_sum(residual, residual)
        direction = residual + norm_next / norm_now * direction
        norm_now = norm_next
    return (solution, residual)


def solution(mesh):
    in_specs = (
        P(None, "row", "col"),
        P(None, "row", "col"),
        P(("row", "col"), None),
        P("col", "row"),
        P(),
        P(),
        P(),
        P(),
    )
    out_specs = (P(("row", "col"), None), P(("row", "col"), None))
    return jax.shard_map(body, mesh=mesh, in_specs=in_specs, out_specs=out_specs, check_vma=False)
```

```python
import functools

import jax
import jax.numpy as jnp
from jax import lax
from jax.experimental import pallas as pl
from jax.experimental.pallas import tpu as pltpu
from jax.sharding import PartitionSpec as P

MESH = pl.DeviceIdType.MESH

DEC = 4
W = 8
ITERS = 4


RIDGE_TERM = 0.1
FULL_PRECISION = lax.Precision.HIGHEST


def extended(cells, sides, width):
    for axis, dim in sides:
        names = axis if isinstance(axis, tuple) else (axis,)
        count = 1
        for name in names:
            count *= lax.axis_size(name)
        head = lax.slice_in_dim(cells, 0, width, axis=dim)
        tail = lax.slice_in_dim(cells, cells.shape[dim] - width, cells.shape[dim], axis=dim)
        cells = jnp.concatenate(
            [
                lax.ppermute(tail, axis, [(i, (i + 1) % count) for i in range(count)]),
                cells,
                lax.ppermute(head, axis, [((i + 1) % count, i) for i in range(count)]),
            ],
            axis=dim,
        )
    return cells


def tap_places(offsets):
    reach = offsets + W
    return reach // DEC, reach % DEC


def blur_down(wide, weights, offsets, rows_out):
    shifts, phases = tap_places(offsets)
    quads = wide.reshape(wide.shape[0] // DEC, DEC, wide.shape[1])
    total = jnp.zeros((rows_out, wide.shape[1]), jnp.float32)
    for number in range(weights.shape[0]):
        piece = lax.dynamic_slice(
            quads, (shifts[number], phases[number], 0), (rows_out, 1, wide.shape[1])
        )[:, 0, :]
        total = total + weights[number] * piece.astype(jnp.float32)
    return total


def blur_up(coarse_wide, weights, offsets, margin):
    shifts, phases = tap_places(offsets)
    rows = coarse_wide.shape[0] - 2 * margin
    columns = coarse_wide.shape[1]
    parts = [jnp.zeros((rows, columns), jnp.float32) for _ in range(DEC)]
    for number in range(weights.shape[0]):
        piece = lax.dynamic_slice_in_dim(coarse_wide, margin + 2 - shifts[number], rows, 0)
        for phase in range(DEC):
            scale = jnp.where(phases[number] == phase, weights[number], jnp.float32(0.0))
            parts[phase] = parts[phase] + scale * piece
    return jnp.stack(parts, axis=1).reshape(rows * DEC, columns)


def total_kernel(rows, cols, part_ref, out_ref, col_held, row_held, sends, receipts):
    here_row = lax.axis_index("row")
    here_col = lax.axis_index("col")
    col_peers = [(here_row, lax.rem(here_col + shift, cols)) for shift in range(1, cols)]
    row_peers = [(lax.rem(here_row + shift, rows), here_col) for shift in range(1, rows)]
    barrier = pltpu.get_barrier_semaphore()
    for peer in col_peers + row_peers:
        pl.semaphore_signal(barrier, inc=1, device_id=peer, device_id_type=MESH)
    pl.semaphore_wait(barrier, len(col_peers) + len(row_peers))
    copies = []
    for number, peer in enumerate(col_peers):
        copy = pltpu.make_async_remote_copy(
            src_ref=part_ref,
            dst_ref=col_held.at[here_col],
            send_sem=sends.at[number],
            recv_sem=receipts.at[number],
            device_id=peer,
            device_id_type=MESH,
        )
        copy.start()
        copies.append(copy)
    col_held[here_col] = part_ref[...]
    for copy in copies:
        copy.wait()
    col_total = col_held[0]
    for source in range(1, cols):
        col_total = col_total + col_held[source]
    row_held[here_row] = col_total
    copies = []
    for number, peer in enumerate(row_peers):
        copy = pltpu.make_async_remote_copy(
            src_ref=row_held.at[here_row],
            dst_ref=row_held.at[here_row],
            send_sem=sends.at[cols + number],
            recv_sem=receipts.at[cols + number],
            device_id=peer,
            device_id_type=MESH,
        )
        copy.start()
        copies.append(copy)
    for copy in copies:
        copy.wait()
    total = row_held[0]
    for source in range(1, rows):
        total = total + row_held[source]
    out_ref[...] = total


def grid_totals(parts):
    rows = lax.axis_size("row")
    cols = lax.axis_size("col")
    lanes = jnp.pad(jnp.stack(parts), (0, 128 - len(parts)))
    tile = jnp.broadcast_to(lanes[None, :], (8, 128))
    summed = pl.pallas_call(
        functools.partial(total_kernel, rows, cols),
        out_shape=jax.ShapeDtypeStruct((8, 128), jnp.float32),
        in_specs=[pl.BlockSpec(memory_space=pltpu.VMEM)],
        out_specs=pl.BlockSpec(memory_space=pltpu.VMEM),
        scratch_shapes=[
            pltpu.VMEM((cols, 8, 128), jnp.float32),
            pltpu.VMEM((rows, 8, 128), jnp.float32),
            pltpu.SemaphoreType.DMA((rows + cols,)),
            pltpu.SemaphoreType.DMA((rows + cols,)),
        ],
        compiler_params=pltpu.CompilerParams(collective_id=0, has_side_effects=True),
    )(tile)
    return [summed[0, number] for number in range(len(parts))]


def scatter_kernel(cols, blocks_ref, gram_ref, sums_ref, grams_ref, held, gram_held, sends, receipts):
    here_row = lax.axis_index("row")
    here_col = lax.axis_index("col")
    peers = [lax.rem(here_col + shift, cols) for shift in range(1, cols)]
    barrier = pltpu.get_barrier_semaphore()
    for peer in peers:
        pl.semaphore_signal(barrier, inc=1, device_id=(here_row, peer), device_id_type=MESH)
    pl.semaphore_wait(barrier, len(peers))
    copies = []
    for number, peer in enumerate(peers):
        for slot, (source, target) in enumerate(
            ((blocks_ref.at[peer], held.at[here_col]), (gram_ref, gram_held.at[here_col]))
        ):
            copy = pltpu.make_async_remote_copy(
                src_ref=source,
                dst_ref=target,
                send_sem=sends.at[2 * number + slot],
                recv_sem=receipts.at[2 * number + slot],
                device_id=(here_row, peer),
                device_id_type=MESH,
            )
            copy.start()
            copies.append(copy)
    held[here_col] = blocks_ref[here_col]
    gram_held[here_col] = gram_ref[...]
    for copy in copies:
        copy.wait()
    sums = held[0]
    grams = gram_held[0]
    for source in range(1, cols):
        sums = sums + held[source]
        grams = grams + gram_held[source]
    sums_ref[...] = sums
    grams_ref[...] = grams


def col_scatter(blocks, gram):
    cols = blocks.shape[0]
    return pl.pallas_call(
        functools.partial(scatter_kernel, cols),
        out_shape=(
            jax.ShapeDtypeStruct(blocks.shape[1:], jnp.float32),
            jax.ShapeDtypeStruct(gram.shape, jnp.float32),
        ),
        in_specs=[pl.BlockSpec(memory_space=pltpu.VMEM)] * 2,
        out_specs=(pl.BlockSpec(memory_space=pltpu.VMEM),) * 2,
        scratch_shapes=[
            pltpu.VMEM(blocks.shape, jnp.float32),
            pltpu.VMEM((cols,) + gram.shape, jnp.float32),
            pltpu.SemaphoreType.DMA((2 * cols,)),
            pltpu.SemaphoreType.DMA((2 * cols,)),
        ],
        compiler_params=pltpu.CompilerParams(collective_id=1, has_side_effects=True),
    )(blocks, gram)


def body(
    multispectral, hyperspectral, row_start, col_factor, band_factor, response, blur_taps, offsets
):
    low_reach = (W + DEC - 1) // DEC
    columns = lax.all_gather(col_factor, "row", axis=1, tiled=True)
    column_wide = extended(columns, (("col", 0),), W)
    coarse_columns = blur_down(column_wide, blur_taps, offsets, columns.shape[0] // DEC)
    merged = jnp.dot(response, band_factor, precision=FULL_PRECISION)
    multi_pairs = (merged[:, None, :] * columns.astype(jnp.float32)[None, :, :]).astype(
        jnp.bfloat16
    )
    hyper_pairs = (band_factor[:, None, :] * coarse_columns[None, :, :]).astype(jnp.bfloat16)
    multi_part = jnp.einsum(
        "kij,kjr->ir", multispectral, multi_pairs, preferred_element_type=jnp.float32
    )
    hyper_part = jnp.einsum(
        "kij,kjr->ir", hyperspectral, hyper_pairs, preferred_element_type=jnp.float32
    )
    column_part = jnp.einsum("jr,js->rs", columns, columns, preferred_element_type=jnp.float32)
    coarse_part = jnp.einsum("jr,js->rs", coarse_columns, coarse_columns, precision=FULL_PRECISION)
    cols = lax.axis_size("col")
    multi_blocks = multi_part.reshape(cols, -1, multi_part.shape[1])
    hyper_blocks = hyper_part.reshape(cols, -1, hyper_part.shape[1])
    joined = jnp.concatenate([multi_blocks, hyper_blocks], axis=1)
    joined, gram_sums = col_scatter(joined, jnp.concatenate([column_part, coarse_part], axis=0))
    column_gram = gram_sums[: column_part.shape[0]]
    coarse_gram = gram_sums[column_part.shape[0] :]
    band_gram = jnp.dot(band_factor.T, band_factor, precision=FULL_PRECISION)
    merged_gram = jnp.dot(merged.T, merged, precision=FULL_PRECISION)
    hyper_gram = coarse_gram * band_gram
    multi_gram = column_gram * merged_gram
    multi_sums = joined[: multi_blocks.shape[1]]
    hyper_sums = joined[multi_blocks.shape[1] :]
    start_rows = row_start
    grid = ("row", "col")

    def inner_sum(first_field, second_field):
        return grid_totals([jnp.sum(first_field * second_field)])[0]

    fine_rows = start_rows.shape[0]
    coarse_rows = fine_rows // DEC
    fine_reach = W + DEC * low_reach

    def operate(values):
        fine_wide = extended(values, ((grid, 0),), fine_reach)
        coarse_wide = blur_down(fine_wide, blur_taps, offsets, coarse_rows + 2 * low_reach)
        restored = blur_up(coarse_wide, blur_taps, offsets, low_reach)
        return (
            jnp.dot(restored, hyper_gram, precision=FULL_PRECISION)
            + jnp.dot(values, multi_gram, precision=FULL_PRECISION)
            + RIDGE_TERM * values
        )

    hyper_wide = extended(hyper_sums, ((grid, 0),), low_reach)
    right_side = blur_up(hyper_wide, blur_taps, offsets, low_reach) + multi_sums
    solution = start_rows
    residual = right_side - operate(solution)
    direction = residual
    norm_now = None
    for iteration in range(ITERS):
        mapped = operate(direction)
        if norm_now is None:
            norm_now, curvature = grid_totals(
                [jnp.sum(residual * residual), jnp.sum(direction * mapped)]
            )
        else:
            curvature = inner_sum(direction, mapped)
        step_size = norm_now / curvature
        solution = solution + step_size * direction
        residual = residual - step_size * mapped
        norm_next = inner_sum(residual, residual)
        direction = residual + norm_next / norm_now * direction
        norm_now = norm_next
    return (solution, residual)


def solution(mesh):
    in_specs = (
        P(None, "row", "col"),
        P(None, "row", "col"),
        P(("row", "col"), None),
        P("col", "row"),
        P(),
        P(),
        P(),
        P(),
    )
    out_specs = (P(("row", "col"), None), P(("row", "col"), None))
    return jax.shard_map(body, mesh=mesh, in_specs=in_specs, out_specs=out_specs, check_vma=False)
```

```python
import functools

import jax
import jax.numpy as jnp
from jax import lax
from jax.experimental import pallas as pl
from jax.experimental.pallas import tpu as pltpu
from jax.sharding import PartitionSpec as P

MESH = pl.DeviceIdType.MESH

DEC = 4
W = 8
ITERS = 4


RIDGE_TERM = 0.1
FULL_PRECISION = lax.Precision.HIGHEST


def extended(cells, sides, width):
    for axis, dim in sides:
        names = axis if isinstance(axis, tuple) else (axis,)
        count = 1
        for name in names:
            count *= lax.axis_size(name)
        head = lax.slice_in_dim(cells, 0, width, axis=dim)
        tail = lax.slice_in_dim(cells, cells.shape[dim] - width, cells.shape[dim], axis=dim)
        cells = jnp.concatenate(
            [
                lax.ppermute(tail, axis, [(i, (i + 1) % count) for i in range(count)]),
                cells,
                lax.ppermute(head, axis, [((i + 1) % count, i) for i in range(count)]),
            ],
            axis=dim,
        )
    return cells


def tap_table(weights, offsets):
    reach = jnp.arange(2 * W + 1, dtype=jnp.int32)
    hits = (offsets[None, :] + W) == reach[:, None]
    return jnp.sum(jnp.where(hits, weights[None, :], jnp.float32(0.0)), axis=1)


def blur_down(wide, table, rows_out):
    quads = wide.reshape(wide.shape[0] // DEC, DEC, wide.shape[1]).astype(jnp.float32)
    total = jnp.zeros((rows_out, wide.shape[1]), jnp.float32)
    for reach in range(2 * W + 1):
        shift, phase = divmod(reach, DEC)
        total = total + table[reach] * quads[shift : shift + rows_out, phase, :]
    return total


def blur_up(coarse_wide, table, margin):
    rows = coarse_wide.shape[0] - 2 * margin
    parts = []
    for phase in range(DEC):
        part = jnp.zeros((rows, coarse_wide.shape[1]), jnp.float32)
        for shift in range((2 * W - phase) // DEC + 1):
            start = margin + 2 - shift
            part = part + table[DEC * shift + phase] * coarse_wide[start : start + rows]
        parts.append(part)
    return jnp.stack(parts, axis=1).reshape(rows * DEC, coarse_wide.shape[1])


def total_kernel(rows, cols, part_ref, out_ref, col_held, row_held, sends, receipts):
    here_row = lax.axis_index("row")
    here_col = lax.axis_index("col")
    col_peers = [(here_row, lax.rem(here_col + shift, cols)) for shift in range(1, cols)]
    row_peers = [(lax.rem(here_row + shift, rows), here_col) for shift in range(1, rows)]
    barrier = pltpu.get_barrier_semaphore()
    for peer in col_peers + row_peers:
        pl.semaphore_signal(barrier, inc=1, device_id=peer, device_id_type=MESH)
    pl.semaphore_wait(barrier, len(col_peers) + len(row_peers))
    copies = []
    for number, peer in enumerate(col_peers):
        copy = pltpu.make_async_remote_copy(
            src_ref=part_ref,
            dst_ref=col_held.at[here_col],
            send_sem=sends.at[number],
            recv_sem=receipts.at[number],
            device_id=peer,
            device_id_type=MESH,
        )
        copy.start()
        copies.append(copy)
    col_held[here_col] = part_ref[...]
    for copy in copies:
        copy.wait()
    col_total = col_held[0]
    for source in range(1, cols):
        col_total = col_total + col_held[source]
    row_held[here_row] = col_total
    copies = []
    for number, peer in enumerate(row_peers):
        copy = pltpu.make_async_remote_copy(
            src_ref=row_held.at[here_row],
            dst_ref=row_held.at[here_row],
            send_sem=sends.at[cols + number],
            recv_sem=receipts.at[cols + number],
            device_id=peer,
            device_id_type=MESH,
        )
        copy.start()
        copies.append(copy)
    for copy in copies:
        copy.wait()
    total = row_held[0]
    for source in range(1, rows):
        total = total + row_held[source]
    out_ref[...] = total


def grid_totals(parts):
    rows = lax.axis_size("row")
    cols = lax.axis_size("col")
    lanes = jnp.pad(jnp.stack(parts), (0, 128 - len(parts)))
    tile = jnp.broadcast_to(lanes[None, :], (8, 128))
    summed = pl.pallas_call(
        functools.partial(total_kernel, rows, cols),
        out_shape=jax.ShapeDtypeStruct((8, 128), jnp.float32),
        in_specs=[pl.BlockSpec(memory_space=pltpu.VMEM)],
        out_specs=pl.BlockSpec(memory_space=pltpu.VMEM),
        scratch_shapes=[
            pltpu.VMEM((cols, 8, 128), jnp.float32),
            pltpu.VMEM((rows, 8, 128), jnp.float32),
            pltpu.SemaphoreType.DMA((rows + cols,)),
            pltpu.SemaphoreType.DMA((rows + cols,)),
        ],
        compiler_params=pltpu.CompilerParams(collective_id=0, has_side_effects=True),
    )(tile)
    return [summed[0, number] for number in range(len(parts))]


def scatter_kernel(cols, blocks_ref, gram_ref, sums_ref, grams_ref, held, gram_held, sends, receipts):
    here_row = lax.axis_index("row")
    here_col = lax.axis_index("col")
    peers = [lax.rem(here_col + shift, cols) for shift in range(1, cols)]
    barrier = pltpu.get_barrier_semaphore()
    for peer in peers:
        pl.semaphore_signal(barrier, inc=1, device_id=(here_row, peer), device_id_type=MESH)
    pl.semaphore_wait(barrier, len(peers))
    copies = []
    for number, peer in enumerate(peers):
        for slot, (source, target) in enumerate(
            ((blocks_ref.at[peer], held.at[here_col]), (gram_ref, gram_held.at[here_col]))
        ):
            copy = pltpu.make_async_remote_copy(
                src_ref=source,
                dst_ref=target,
                send_sem=sends.at[2 * number + slot],
                recv_sem=receipts.at[2 * number + slot],
                device_id=(here_row, peer),
                device_id_type=MESH,
            )
            copy.start()
            copies.append(copy)
    held[here_col] = blocks_ref[here_col]
    gram_held[here_col] = gram_ref[...]
    for copy in copies:
        copy.wait()
    sums = held[0]
    grams = gram_held[0]
    for source in range(1, cols):
        sums = sums + held[source]
        grams = grams + gram_held[source]
    sums_ref[...] = sums
    grams_ref[...] = grams


def col_scatter(blocks, gram):
    cols = blocks.shape[0]
    return pl.pallas_call(
        functools.partial(scatter_kernel, cols),
        out_shape=(
            jax.ShapeDtypeStruct(blocks.shape[1:], jnp.float32),
            jax.ShapeDtypeStruct(gram.shape, jnp.float32),
        ),
        in_specs=[pl.BlockSpec(memory_space=pltpu.VMEM)] * 2,
        out_specs=(pl.BlockSpec(memory_space=pltpu.VMEM),) * 2,
        scratch_shapes=[
            pltpu.VMEM(blocks.shape, jnp.float32),
            pltpu.VMEM((cols,) + gram.shape, jnp.float32),
            pltpu.SemaphoreType.DMA((2 * cols,)),
            pltpu.SemaphoreType.DMA((2 * cols,)),
        ],
        compiler_params=pltpu.CompilerParams(collective_id=1, has_side_effects=True),
    )(blocks, gram)


def body(
    multispectral, hyperspectral, row_start, col_factor, band_factor, response, blur_taps, offsets
):
    low_reach = (W + DEC - 1) // DEC
    table = tap_table(blur_taps, offsets)
    columns = lax.all_gather(col_factor, "row", axis=1, tiled=True)
    column_wide = extended(columns, (("col", 0),), W)
    coarse_columns = blur_down(column_wide, table, columns.shape[0] // DEC)
    merged = jnp.dot(response, band_factor, precision=FULL_PRECISION)
    multi_pairs = (merged[:, None, :] * columns.astype(jnp.float32)[None, :, :]).astype(
        jnp.bfloat16
    )
    hyper_pairs = (band_factor[:, None, :] * coarse_columns[None, :, :]).astype(jnp.bfloat16)
    multi_part = jnp.einsum(
        "kij,kjr->ir", multispectral, multi_pairs, preferred_element_type=jnp.float32
    )
    hyper_part = jnp.einsum(
        "kij,kjr->ir", hyperspectral, hyper_pairs, preferred_element_type=jnp.float32
    )
    column_part = jnp.einsum("jr,js->rs", columns, columns, preferred_element_type=jnp.float32)
    coarse_part = jnp.einsum("jr,js->rs", coarse_columns, coarse_columns, precision=FULL_PRECISION)
    cols = lax.axis_size("col")
    multi_blocks = multi_part.reshape(cols, -1, multi_part.shape[1])
    hyper_blocks = hyper_part.reshape(cols, -1, hyper_part.shape[1])
    joined = jnp.concatenate([multi_blocks, hyper_blocks], axis=1)
    joined, gram_sums = col_scatter(joined, jnp.concatenate([column_part, coarse_part], axis=0))
    column_gram = gram_sums[: column_part.shape[0]]
    coarse_gram = gram_sums[column_part.shape[0] :]
    band_gram = jnp.dot(band_factor.T, band_factor, precision=FULL_PRECISION)
    merged_gram = jnp.dot(merged.T, merged, precision=FULL_PRECISION)
    hyper_gram = coarse_gram * band_gram
    multi_gram = column_gram * merged_gram
    multi_sums = joined[: multi_blocks.shape[1]]
    hyper_sums = joined[multi_blocks.shape[1] :]
    start_rows = row_start
    grid = ("row", "col")

    def inner_sum(first_field, second_field):
        return grid_totals([jnp.sum(first_field * second_field)])[0]

    fine_rows = start_rows.shape[0]
    coarse_rows = fine_rows // DEC
    fine_reach = W + DEC * low_reach

    def operate(values):
        fine_wide = extended(values, ((grid, 0),), fine_reach)
        coarse_wide = blur_down(fine_wide, table, coarse_rows + 2 * low_reach)
        restored = blur_up(coarse_wide, table, low_reach)
        return (
            jnp.dot(restored, hyper_gram, precision=FULL_PRECISION)
            + jnp.dot(values, multi_gram, precision=FULL_PRECISION)
            + RIDGE_TERM * values
        )

    hyper_wide = extended(hyper_sums, ((grid, 0),), low_reach)
    right_side = blur_up(hyper_wide, table, low_reach) + multi_sums
    solution = start_rows
    residual = right_side - operate(solution)
    direction = residual
    norm_now = None
    for iteration in range(ITERS):
        mapped = operate(direction)
        if norm_now is None:
            norm_now, curvature = grid_totals(
                [jnp.sum(residual * residual), jnp.sum(direction * mapped)]
            )
        else:
            curvature = inner_sum(direction, mapped)
        step_size = norm_now / curvature
        solution = solution + step_size * direction
        residual = residual - step_size * mapped
        norm_next = inner_sum(residual, residual)
        direction = residual + norm_next / norm_now * direction
        norm_now = norm_next
    return (solution, residual)


def solution(mesh):
    in_specs = (
        P(None, "row", "col"),
        P(None, "row", "col"),
        P(("row", "col"), None),
        P("col", "row"),
        P(),
        P(),
        P(),
        P(),
    )
    out_specs = (P(("row", "col"), None), P(("row", "col"), None))
    return jax.shard_map(body, mesh=mesh, in_specs=in_specs, out_specs=out_specs, check_vma=False)
```

```python
import functools

import jax
import jax.numpy as jnp
from jax import lax
from jax.experimental import pallas as pl
from jax.experimental.pallas import tpu as pltpu
from jax.sharding import PartitionSpec as P

MESH = pl.DeviceIdType.MESH

DEC = 4
W = 8
ITERS = 4


RIDGE_TERM = 0.1
FULL_PRECISION = lax.Precision.HIGHEST


def extended(cells, sides, width):
    for axis, dim in sides:
        names = axis if isinstance(axis, tuple) else (axis,)
        count = 1
        for name in names:
            count *= lax.axis_size(name)
        head = lax.slice_in_dim(cells, 0, width, axis=dim)
        tail = lax.slice_in_dim(cells, cells.shape[dim] - width, cells.shape[dim], axis=dim)
        cells = jnp.concatenate(
            [
                lax.ppermute(tail, axis, [(i, (i + 1) % count) for i in range(count)]),
                cells,
                lax.ppermute(head, axis, [((i + 1) % count, i) for i in range(count)]),
            ],
            axis=dim,
        )
    return cells


def down_matrix(weights, offsets, rows_out, rows_in):
    outer = lax.broadcasted_iota(jnp.int32, (rows_out, rows_in, 1), 0)
    inner = lax.broadcasted_iota(jnp.int32, (rows_out, rows_in, 1), 1)
    hits = inner == DEC * outer + offsets[None, None, :] + W
    return jnp.sum(jnp.where(hits, weights[None, None, :], jnp.float32(0.0)), axis=2)


def up_matrix(weights, offsets, rows_in, low_margin):
    rows_out = (rows_in - 2 * low_margin) * DEC
    outer = lax.broadcasted_iota(jnp.int32, (rows_out, rows_in, 1), 0)
    inner = lax.broadcasted_iota(jnp.int32, (rows_out, rows_in, 1), 1)
    hits = DEC * inner == outer + DEC * low_margin - offsets[None, None, :]
    return jnp.sum(jnp.where(hits, weights[None, None, :], jnp.float32(0.0)), axis=2)


def apply_band(matrix, values):
    return jnp.dot(matrix, values.astype(jnp.float32), precision=FULL_PRECISION)


def total_kernel(rows, cols, part_ref, out_ref, col_held, row_held, sends, receipts):
    here_row = lax.axis_index("row")
    here_col = lax.axis_index("col")
    col_peers = [(here_row, lax.rem(here_col + shift, cols)) for shift in range(1, cols)]
    row_peers = [(lax.rem(here_row + shift, rows), here_col) for shift in range(1, rows)]
    barrier = pltpu.get_barrier_semaphore()
    for peer in col_peers + row_peers:
        pl.semaphore_signal(barrier, inc=1, device_id=peer, device_id_type=MESH)
    pl.semaphore_wait(barrier, len(col_peers) + len(row_peers))
    copies = []
    for number, peer in enumerate(col_peers):
        copy = pltpu.make_async_remote_copy(
            src_ref=part_ref,
            dst_ref=col_held.at[here_col],
            send_sem=sends.at[number],
            recv_sem=receipts.at[number],
            device_id=peer,
            device_id_type=MESH,
        )
        copy.start()
        copies.append(copy)
    col_held[here_col] = part_ref[...]
    for copy in copies:
        copy.wait()
    col_total = col_held[0]
    for source in range(1, cols):
        col_total = col_total + col_held[source]
    row_held[here_row] = col_total
    copies = []
    for number, peer in enumerate(row_peers):
        copy = pltpu.make_async_remote_copy(
            src_ref=row_held.at[here_row],
            dst_ref=row_held.at[here_row],
            send_sem=sends.at[cols + number],
            recv_sem=receipts.at[cols + number],
            device_id=peer,
            device_id_type=MESH,
        )
        copy.start()
        copies.append(copy)
    for copy in copies:
        copy.wait()
    total = row_held[0]
    for source in range(1, rows):
        total = total + row_held[source]
    out_ref[...] = total


def grid_totals(parts):
    rows = lax.axis_size("row")
    cols = lax.axis_size("col")
    lanes = jnp.pad(jnp.stack(parts), (0, 128 - len(parts)))
    tile = jnp.broadcast_to(lanes[None, :], (8, 128))
    summed = pl.pallas_call(
        functools.partial(total_kernel, rows, cols),
        out_shape=jax.ShapeDtypeStruct((8, 128), jnp.float32),
        in_specs=[pl.BlockSpec(memory_space=pltpu.VMEM)],
        out_specs=pl.BlockSpec(memory_space=pltpu.VMEM),
        scratch_shapes=[
            pltpu.VMEM((cols, 8, 128), jnp.float32),
            pltpu.VMEM((rows, 8, 128), jnp.float32),
            pltpu.SemaphoreType.DMA((rows + cols,)),
            pltpu.SemaphoreType.DMA((rows + cols,)),
        ],
        compiler_params=pltpu.CompilerParams(collective_id=0, has_side_effects=True),
    )(tile)
    return [summed[0, number] for number in range(len(parts))]


def scatter_kernel(cols, blocks_ref, gram_ref, sums_ref, grams_ref, held, gram_held, sends, receipts):
    here_row = lax.axis_index("row")
    here_col = lax.axis_index("col")
    peers = [lax.rem(here_col + shift, cols) for shift in range(1, cols)]
    barrier = pltpu.get_barrier_semaphore()
    for peer in peers:
        pl.semaphore_signal(barrier, inc=1, device_id=(here_row, peer), device_id_type=MESH)
    pl.semaphore_wait(barrier, len(peers))
    copies = []
    for number, peer in enumerate(peers):
        for slot, (source, target) in enumerate(
            ((blocks_ref.at[peer], held.at[here_col]), (gram_ref, gram_held.at[here_col]))
        ):
            copy = pltpu.make_async_remote_copy(
                src_ref=source,
                dst_ref=target,
                send_sem=sends.at[2 * number + slot],
                recv_sem=receipts.at[2 * number + slot],
                device_id=(here_row, peer),
                device_id_type=MESH,
            )
            copy.start()
            copies.append(copy)
    held[here_col] = blocks_ref[here_col]
    gram_held[here_col] = gram_ref[...]
    for copy in copies:
        copy.wait()
    sums = held[0]
    grams = gram_held[0]
    for source in range(1, cols):
        sums = sums + held[source]
        grams = grams + gram_held[source]
    sums_ref[...] = sums
    grams_ref[...] = grams


def col_scatter(blocks, gram):
    cols = blocks.shape[0]
    return pl.pallas_call(
        functools.partial(scatter_kernel, cols),
        out_shape=(
            jax.ShapeDtypeStruct(blocks.shape[1:], jnp.float32),
            jax.ShapeDtypeStruct(gram.shape, jnp.float32),
        ),
        in_specs=[pl.BlockSpec(memory_space=pltpu.VMEM)] * 2,
        out_specs=(pl.BlockSpec(memory_space=pltpu.VMEM),) * 2,
        scratch_shapes=[
            pltpu.VMEM(blocks.shape, jnp.float32),
            pltpu.VMEM((cols,) + gram.shape, jnp.float32),
            pltpu.SemaphoreType.DMA((2 * cols,)),
            pltpu.SemaphoreType.DMA((2 * cols,)),
        ],
        compiler_params=pltpu.CompilerParams(collective_id=1, has_side_effects=True),
    )(blocks, gram)


def body(
    multispectral, hyperspectral, row_start, col_factor, band_factor, response, blur_taps, offsets
):
    low_reach = (W + DEC - 1) // DEC
    columns = lax.all_gather(col_factor, "row", axis=1, tiled=True)
    column_wide = extended(columns, (("col", 0),), W)
    column_down = down_matrix(blur_taps, offsets, columns.shape[0] // DEC, column_wide.shape[0])
    coarse_columns = apply_band(column_down, column_wide)
    merged = jnp.dot(response, band_factor, precision=FULL_PRECISION)
    multi_pairs = (merged[:, None, :] * columns.astype(jnp.float32)[None, :, :]).astype(
        jnp.bfloat16
    )
    hyper_pairs = (band_factor[:, None, :] * coarse_columns[None, :, :]).astype(jnp.bfloat16)
    multi_part = jnp.einsum(
        "kij,kjr->ir", multispectral, multi_pairs, preferred_element_type=jnp.float32
    )
    hyper_part = jnp.einsum(
        "kij,kjr->ir", hyperspectral, hyper_pairs, preferred_element_type=jnp.float32
    )
    column_part = jnp.einsum("jr,js->rs", columns, columns, preferred_element_type=jnp.float32)
    coarse_part = jnp.einsum("jr,js->rs", coarse_columns, coarse_columns, precision=FULL_PRECISION)
    cols = lax.axis_size("col")
    multi_blocks = multi_part.reshape(cols, -1, multi_part.shape[1])
    hyper_blocks = hyper_part.reshape(cols, -1, hyper_part.shape[1])
    joined = jnp.concatenate([multi_blocks, hyper_blocks], axis=1)
    joined, gram_sums = col_scatter(joined, jnp.concatenate([column_part, coarse_part], axis=0))
    column_gram = gram_sums[: column_part.shape[0]]
    coarse_gram = gram_sums[column_part.shape[0] :]
    band_gram = jnp.dot(band_factor.T, band_factor, precision=FULL_PRECISION)
    merged_gram = jnp.dot(merged.T, merged, precision=FULL_PRECISION)
    hyper_gram = coarse_gram * band_gram
    multi_gram = column_gram * merged_gram
    multi_sums = joined[: multi_blocks.shape[1]]
    hyper_sums = joined[multi_blocks.shape[1] :]
    start_rows = row_start
    grid = ("row", "col")

    def inner_sum(first_field, second_field):
        return grid_totals([jnp.sum(first_field * second_field)])[0]

    fine_rows = start_rows.shape[0]
    coarse_rows = fine_rows // DEC
    fine_reach = W + DEC * low_reach

    lifting = up_matrix(blur_taps, offsets, coarse_rows + 2 * low_reach, low_reach)
    lowering = down_matrix(blur_taps, offsets, coarse_rows + 2 * low_reach, fine_rows + 2 * fine_reach)
    blurring = jnp.dot(lifting, lowering, precision=FULL_PRECISION)

    def operate(values):
        fine_wide = extended(values, ((grid, 0),), fine_reach)
        restored = apply_band(blurring, fine_wide)
        return (
            jnp.dot(restored, hyper_gram, precision=FULL_PRECISION)
            + jnp.dot(values, multi_gram, precision=FULL_PRECISION)
            + RIDGE_TERM * values
        )

    hyper_wide = extended(hyper_sums, ((grid, 0),), low_reach)
    right_side = apply_band(lifting, hyper_wide) + multi_sums
    solution = start_rows
    residual = right_side - operate(solution)
    direction = residual
    norm_now = None
    for iteration in range(ITERS):
        mapped = operate(direction)
        if norm_now is None:
            norm_now, curvature = grid_totals(
                [jnp.sum(residual * residual), jnp.sum(direction * mapped)]
            )
        else:
            curvature = inner_sum(direction, mapped)
        step_size = norm_now / curvature
        solution = solution + step_size * direction
        residual = residual - step_size * mapped
        norm_next = inner_sum(residual, residual)
        direction = residual + norm_next / norm_now * direction
        norm_now = norm_next
    return (solution, residual)


def solution(mesh):
    in_specs = (
        P(None, "row", "col"),
        P(None, "row", "col"),
        P(("row", "col"), None),
        P("col", "row"),
        P(),
        P(),
        P(),
        P(),
    )
    out_specs = (P(("row", "col"), None), P(("row", "col"), None))
    return jax.shard_map(body, mesh=mesh, in_specs=in_specs, out_specs=out_specs, check_vma=False)
```

```python
import functools

import jax
import jax.numpy as jnp
from jax import lax
from jax.experimental import pallas as pl
from jax.experimental.pallas import tpu as pltpu
from jax.sharding import PartitionSpec as P

MESH = pl.DeviceIdType.MESH

DEC = 4
W = 8
ITERS = 4


RIDGE_TERM = 0.1
FULL_PRECISION = lax.Precision.HIGHEST


def extended(cells, sides, width):
    for axis, dim in sides:
        names = axis if isinstance(axis, tuple) else (axis,)
        count = 1
        for name in names:
            count *= lax.axis_size(name)
        head = lax.slice_in_dim(cells, 0, width, axis=dim)
        tail = lax.slice_in_dim(cells, cells.shape[dim] - width, cells.shape[dim], axis=dim)
        cells = jnp.concatenate(
            [
                lax.ppermute(tail, axis, [(i, (i + 1) % count) for i in range(count)]),
                cells,
                lax.ppermute(head, axis, [((i + 1) % count, i) for i in range(count)]),
            ],
            axis=dim,
        )
    return cells


def down_matrix(weights, offsets, rows_out, rows_in):
    outer = lax.broadcasted_iota(jnp.int32, (rows_out, rows_in, 1), 0)
    inner = lax.broadcasted_iota(jnp.int32, (rows_out, rows_in, 1), 1)
    hits = inner == DEC * outer + offsets[None, None, :] + W
    return jnp.sum(jnp.where(hits, weights[None, None, :], jnp.float32(0.0)), axis=2)


def up_matrix(weights, offsets, rows_in, low_margin):
    rows_out = (rows_in - 2 * low_margin) * DEC
    outer = lax.broadcasted_iota(jnp.int32, (rows_out, rows_in, 1), 0)
    inner = lax.broadcasted_iota(jnp.int32, (rows_out, rows_in, 1), 1)
    hits = DEC * inner == outer + DEC * low_margin - offsets[None, None, :]
    return jnp.sum(jnp.where(hits, weights[None, None, :], jnp.float32(0.0)), axis=2)


def apply_band(matrix, values):
    return jnp.dot(matrix, values.astype(jnp.float32), precision=FULL_PRECISION)


def total_kernel(rows, cols, part_ref, out_ref, col_held, row_held, sends, receipts):
    here_row = lax.axis_index("row")
    here_col = lax.axis_index("col")
    col_peers = [(here_row, lax.rem(here_col + shift, cols)) for shift in range(1, cols)]
    row_peers = [(lax.rem(here_row + shift, rows), here_col) for shift in range(1, rows)]
    barrier = pltpu.get_barrier_semaphore()
    for peer in col_peers + row_peers:
        pl.semaphore_signal(barrier, inc=1, device_id=peer, device_id_type=MESH)
    pl.semaphore_wait(barrier, len(col_peers) + len(row_peers))
    copies = []
    for number, peer in enumerate(col_peers):
        copy = pltpu.make_async_remote_copy(
            src_ref=part_ref,
            dst_ref=col_held.at[here_col],
            send_sem=sends.at[number],
            recv_sem=receipts.at[number],
            device_id=peer,
            device_id_type=MESH,
        )
        copy.start()
        copies.append(copy)
    col_held[here_col] = part_ref[...]
    for copy in copies:
        copy.wait()
    col_total = col_held[0]
    for source in range(1, cols):
        col_total = col_total + col_held[source]
    row_held[here_row] = col_total
    copies = []
    for number, peer in enumerate(row_peers):
        copy = pltpu.make_async_remote_copy(
            src_ref=row_held.at[here_row],
            dst_ref=row_held.at[here_row],
            send_sem=sends.at[cols + number],
            recv_sem=receipts.at[cols + number],
            device_id=peer,
            device_id_type=MESH,
        )
        copy.start()
        copies.append(copy)
    for copy in copies:
        copy.wait()
    total = row_held[0]
    for source in range(1, rows):
        total = total + row_held[source]
    out_ref[...] = total


def grid_totals(parts):
    rows = lax.axis_size("row")
    cols = lax.axis_size("col")
    lanes = jnp.pad(jnp.stack(parts), (0, 128 - len(parts)))
    tile = jnp.broadcast_to(lanes[None, :], (8, 128))
    summed = pl.pallas_call(
        functools.partial(total_kernel, rows, cols),
        out_shape=jax.ShapeDtypeStruct((8, 128), jnp.float32),
        in_specs=[pl.BlockSpec(memory_space=pltpu.VMEM)],
        out_specs=pl.BlockSpec(memory_space=pltpu.VMEM),
        scratch_shapes=[
            pltpu.VMEM((cols, 8, 128), jnp.float32),
            pltpu.VMEM((rows, 8, 128), jnp.float32),
            pltpu.SemaphoreType.DMA((rows + cols,)),
            pltpu.SemaphoreType.DMA((rows + cols,)),
        ],
        compiler_params=pltpu.CompilerParams(collective_id=0, has_side_effects=True),
    )(tile)
    return [summed[0, number] for number in range(len(parts))]


def scatter_kernel(cols, blocks_ref, gram_ref, sums_ref, grams_ref, held, gram_held, sends, receipts):
    here_row = lax.axis_index("row")
    here_col = lax.axis_index("col")
    peers = [lax.rem(here_col + shift, cols) for shift in range(1, cols)]
    barrier = pltpu.get_barrier_semaphore()
    for peer in peers:
        pl.semaphore_signal(barrier, inc=1, device_id=(here_row, peer), device_id_type=MESH)
    pl.semaphore_wait(barrier, len(peers))
    copies = []
    for number, peer in enumerate(peers):
        for slot, (source, target) in enumerate(
            ((blocks_ref.at[peer], held.at[here_col]), (gram_ref, gram_held.at[here_col]))
        ):
            copy = pltpu.make_async_remote_copy(
                src_ref=source,
                dst_ref=target,
                send_sem=sends.at[2 * number + slot],
                recv_sem=receipts.at[2 * number + slot],
                device_id=(here_row, peer),
                device_id_type=MESH,
            )
            copy.start()
            copies.append(copy)
    held[here_col] = blocks_ref[here_col]
    gram_held[here_col] = gram_ref[...]
    for copy in copies:
        copy.wait()
    sums = held[0]
    grams = gram_held[0]
    for source in range(1, cols):
        sums = sums + held[source]
        grams = grams + gram_held[source]
    sums_ref[...] = sums
    grams_ref[...] = grams


def col_scatter(blocks, gram):
    cols = blocks.shape[0]
    return pl.pallas_call(
        functools.partial(scatter_kernel, cols),
        out_shape=(
            jax.ShapeDtypeStruct(blocks.shape[1:], jnp.float32),
            jax.ShapeDtypeStruct(gram.shape, jnp.float32),
        ),
        in_specs=[pl.BlockSpec(memory_space=pltpu.VMEM)] * 2,
        out_specs=(pl.BlockSpec(memory_space=pltpu.VMEM),) * 2,
        scratch_shapes=[
            pltpu.VMEM(blocks.shape, jnp.float32),
            pltpu.VMEM((cols,) + gram.shape, jnp.float32),
            pltpu.SemaphoreType.DMA((2 * cols,)),
            pltpu.SemaphoreType.DMA((2 * cols,)),
        ],
        compiler_params=pltpu.CompilerParams(collective_id=1, has_side_effects=True),
    )(blocks, gram)


def body(
    multispectral, hyperspectral, row_start, col_factor, band_factor, response, blur_taps, offsets
):
    low_reach = (W + DEC - 1) // DEC
    columns = lax.all_gather(col_factor, "row", axis=1, tiled=True)
    column_wide = extended(columns, (("col", 0),), W)
    column_down = down_matrix(blur_taps, offsets, columns.shape[0] // DEC, column_wide.shape[0])
    coarse_columns = apply_band(column_down, column_wide)
    merged = jnp.dot(response, band_factor, precision=FULL_PRECISION)
    multi_pairs = (merged[:, None, :] * columns.astype(jnp.float32)[None, :, :]).astype(
        jnp.bfloat16
    )
    hyper_pairs = (band_factor[:, None, :] * coarse_columns[None, :, :]).astype(jnp.bfloat16)
    multi_part = jnp.einsum(
        "kij,kjr->ir", multispectral, multi_pairs, preferred_element_type=jnp.float32
    )
    hyper_part = jnp.einsum(
        "kij,kjr->ir", hyperspectral, hyper_pairs, preferred_element_type=jnp.float32
    )
    column_part = jnp.einsum("jr,js->rs", columns, columns, preferred_element_type=jnp.float32)
    coarse_part = jnp.einsum("jr,js->rs", coarse_columns, coarse_columns, precision=FULL_PRECISION)
    cols = lax.axis_size("col")
    multi_blocks = multi_part.reshape(cols, -1, multi_part.shape[1])
    hyper_blocks = hyper_part.reshape(cols, -1, hyper_part.shape[1])
    joined = jnp.concatenate([multi_blocks, hyper_blocks], axis=1)
    joined, gram_sums = col_scatter(joined, jnp.concatenate([column_part, coarse_part], axis=0))
    column_gram = gram_sums[: column_part.shape[0]]
    coarse_gram = gram_sums[column_part.shape[0] :]
    band_gram = jnp.dot(band_factor.T, band_factor, precision=FULL_PRECISION)
    merged_gram = jnp.dot(merged.T, merged, precision=FULL_PRECISION)
    hyper_gram = coarse_gram * band_gram
    multi_gram = column_gram * merged_gram
    multi_sums = joined[: multi_blocks.shape[1]]
    hyper_sums = joined[multi_blocks.shape[1] :]
    start_rows = row_start
    grid = ("row", "col")

    fine_rows = start_rows.shape[0]
    fine_reach = W + DEC * low_reach
    halo = (ITERS + 1) * fine_reach
    coarse_halo = halo // DEC + low_reach
    wide_rows = fine_rows + 2 * halo
    count = lax.axis_size("row") * cols
    pieces = (start_rows, multi_sums, hyper_sums)
    reaches = (halo, halo, coarse_halo)
    tails = jnp.concatenate([piece[piece.shape[0] - reach :] for piece, reach in zip(pieces, reaches)])
    heads = jnp.concatenate([piece[:reach] for piece, reach in zip(pieces, reaches)])
    before = lax.ppermute(tails, grid, [(i, (i + 1) % count) for i in range(count)])
    after = lax.ppermute(heads, grid, [((i + 1) % count, i) for i in range(count)])
    wide = []
    corner = 0
    for piece, reach in zip(pieces, reaches):
        wide.append(
            jnp.concatenate(
                [before[corner : corner + reach], piece, after[corner : corner + reach]]
            )
        )
        corner += reach
    start_wide, multi_wide, hyper_wide = wide

    lifting = up_matrix(blur_taps, offsets, wide_rows // DEC + 2 * low_reach, low_reach)
    lowering = down_matrix(
        blur_taps, offsets, wide_rows // DEC + 2 * low_reach, wide_rows + 2 * fine_reach
    )
    blurring = jnp.dot(lifting, lowering, precision=FULL_PRECISION)
    blurring = blurring[:, fine_reach : fine_reach + wide_rows]

    def operate(values):
        restored = apply_band(blurring, values)
        return (
            jnp.dot(restored, hyper_gram, precision=FULL_PRECISION)
            + jnp.dot(values, multi_gram, precision=FULL_PRECISION)
            + RIDGE_TERM * values
        )

    def own(values):
        return values[halo : halo + fine_rows]

    def inner_sum(first_field, second_field):
        return grid_totals([jnp.sum(own(first_field) * own(second_field))])[0]

    right_side = apply_band(lifting, hyper_wide) + multi_wide
    solution = start_wide
    residual = right_side - operate(solution)
    direction = residual
    norm_now = None
    for iteration in range(ITERS):
        mapped = operate(direction)
        if norm_now is None:
            norm_now, curvature = grid_totals(
                [jnp.sum(own(residual) * own(residual)), jnp.sum(own(direction) * own(mapped))]
            )
        else:
            curvature = inner_sum(direction, mapped)
        step_size = norm_now / curvature
        solution = solution + step_size * direction
        residual = residual - step_size * mapped
        norm_next = inner_sum(residual, residual)
        direction = residual + norm_next / norm_now * direction
        norm_now = norm_next
    solution = own(solution)
    residual = own(residual)
    return (solution, residual)


def solution(mesh):
    in_specs = (
        P(None, "row", "col"),
        P(None, "row", "col"),
        P(("row", "col"), None),
        P("col", "row"),
        P(),
        P(),
        P(),
        P(),
    )
    out_specs = (P(("row", "col"), None), P(("row", "col"), None))
    return jax.shard_map(body, mesh=mesh, in_specs=in_specs, out_specs=out_specs, check_vma=False)
```

```python
import functools

import jax
import jax.numpy as jnp
from jax import lax
from jax.experimental import pallas as pl
from jax.experimental.pallas import tpu as pltpu
from jax.sharding import PartitionSpec as P

MESH = pl.DeviceIdType.MESH

DEC = 4
W = 8
ITERS = 4


RIDGE_TERM = 0.1
FULL_PRECISION = lax.Precision.HIGHEST


def extended(cells, sides, width):
    for axis, dim in sides:
        names = axis if isinstance(axis, tuple) else (axis,)
        count = 1
        for name in names:
            count *= lax.axis_size(name)
        head = lax.slice_in_dim(cells, 0, width, axis=dim)
        tail = lax.slice_in_dim(cells, cells.shape[dim] - width, cells.shape[dim], axis=dim)
        cells = jnp.concatenate(
            [
                lax.ppermute(tail, axis, [(i, (i + 1) % count) for i in range(count)]),
                cells,
                lax.ppermute(head, axis, [((i + 1) % count, i) for i in range(count)]),
            ],
            axis=dim,
        )
    return cells


def down_matrix(weights, offsets, rows_out, rows_in):
    outer = lax.broadcasted_iota(jnp.int32, (rows_out, rows_in, 1), 0)
    inner = lax.broadcasted_iota(jnp.int32, (rows_out, rows_in, 1), 1)
    hits = inner == DEC * outer + offsets[None, None, :] + W
    return jnp.sum(jnp.where(hits, weights[None, None, :], jnp.float32(0.0)), axis=2)


def up_matrix(weights, offsets, rows_in, low_margin):
    rows_out = (rows_in - 2 * low_margin) * DEC
    outer = lax.broadcasted_iota(jnp.int32, (rows_out, rows_in, 1), 0)
    inner = lax.broadcasted_iota(jnp.int32, (rows_out, rows_in, 1), 1)
    hits = DEC * inner == outer + DEC * low_margin - offsets[None, None, :]
    return jnp.sum(jnp.where(hits, weights[None, None, :], jnp.float32(0.0)), axis=2)


def apply_band(matrix, values):
    return jnp.dot(matrix, values.astype(jnp.float32), precision=FULL_PRECISION)


def total_kernel(rows, cols, part_ref, out_ref, col_held, row_held, sends, receipts):
    here_row = lax.axis_index("row")
    here_col = lax.axis_index("col")
    col_peers = [(here_row, lax.rem(here_col + shift, cols)) for shift in range(1, cols)]
    row_peers = [(lax.rem(here_row + shift, rows), here_col) for shift in range(1, rows)]
    barrier = pltpu.get_barrier_semaphore()
    for peer in col_peers + row_peers:
        pl.semaphore_signal(barrier, inc=1, device_id=peer, device_id_type=MESH)
    pl.semaphore_wait(barrier, len(col_peers) + len(row_peers))
    copies = []
    for number, peer in enumerate(col_peers):
        copy = pltpu.make_async_remote_copy(
            src_ref=part_ref,
            dst_ref=col_held.at[here_col],
            send_sem=sends.at[number],
            recv_sem=receipts.at[number],
            device_id=peer,
            device_id_type=MESH,
        )
        copy.start()
        copies.append(copy)
    col_held[here_col] = part_ref[...]
    for copy in copies:
        copy.wait()
    col_total = col_held[0]
    for source in range(1, cols):
        col_total = col_total + col_held[source]
    row_held[here_row] = col_total
    copies = []
    for number, peer in enumerate(row_peers):
        copy = pltpu.make_async_remote_copy(
            src_ref=row_held.at[here_row],
            dst_ref=row_held.at[here_row],
            send_sem=sends.at[cols + number],
            recv_sem=receipts.at[cols + number],
            device_id=peer,
            device_id_type=MESH,
        )
        copy.start()
        copies.append(copy)
    for copy in copies:
        copy.wait()
    total = row_held[0]
    for source in range(1, rows):
        total = total + row_held[source]
    out_ref[...] = total


def grid_totals(parts):
    rows = lax.axis_size("row")
    cols = lax.axis_size("col")
    lanes = jnp.pad(jnp.stack(parts), (0, 128 - len(parts)))
    tile = jnp.broadcast_to(lanes[None, :], (8, 128))
    summed = pl.pallas_call(
        functools.partial(total_kernel, rows, cols),
        out_shape=jax.ShapeDtypeStruct((8, 128), jnp.float32),
        in_specs=[pl.BlockSpec(memory_space=pltpu.VMEM)],
        out_specs=pl.BlockSpec(memory_space=pltpu.VMEM),
        scratch_shapes=[
            pltpu.VMEM((cols, 8, 128), jnp.float32),
            pltpu.VMEM((rows, 8, 128), jnp.float32),
            pltpu.SemaphoreType.DMA((rows + cols,)),
            pltpu.SemaphoreType.DMA((rows + cols,)),
        ],
        compiler_params=pltpu.CompilerParams(collective_id=0, has_side_effects=True),
    )(tile)
    return [summed[0, number] for number in range(len(parts))]


def scatter_kernel(cols, blocks_ref, gram_ref, sums_ref, grams_ref, held, gram_held, sends, receipts):
    here_row = lax.axis_index("row")
    here_col = lax.axis_index("col")
    peers = [lax.rem(here_col + shift, cols) for shift in range(1, cols)]
    barrier = pltpu.get_barrier_semaphore()
    for peer in peers:
        pl.semaphore_signal(barrier, inc=1, device_id=(here_row, peer), device_id_type=MESH)
    pl.semaphore_wait(barrier, len(peers))
    copies = []
    for number, peer in enumerate(peers):
        for slot, (source, target) in enumerate(
            ((blocks_ref.at[peer], held.at[here_col]), (gram_ref, gram_held.at[here_col]))
        ):
            copy = pltpu.make_async_remote_copy(
                src_ref=source,
                dst_ref=target,
                send_sem=sends.at[2 * number + slot],
                recv_sem=receipts.at[2 * number + slot],
                device_id=(here_row, peer),
                device_id_type=MESH,
            )
            copy.start()
            copies.append(copy)
    held[here_col] = blocks_ref[here_col]
    gram_held[here_col] = gram_ref[...]
    for copy in copies:
        copy.wait()
    sums = held[0]
    grams = gram_held[0]
    for source in range(1, cols):
        sums = sums + held[source]
        grams = grams + gram_held[source]
    sums_ref[...] = sums
    grams_ref[...] = grams


def col_scatter(blocks, gram):
    cols = blocks.shape[0]
    return pl.pallas_call(
        functools.partial(scatter_kernel, cols),
        out_shape=(
            jax.ShapeDtypeStruct(blocks.shape[1:], jnp.float32),
            jax.ShapeDtypeStruct(gram.shape, jnp.float32),
        ),
        in_specs=[pl.BlockSpec(memory_space=pltpu.VMEM)] * 2,
        out_specs=(pl.BlockSpec(memory_space=pltpu.VMEM),) * 2,
        scratch_shapes=[
            pltpu.VMEM(blocks.shape, jnp.float32),
            pltpu.VMEM((cols,) + gram.shape, jnp.float32),
            pltpu.SemaphoreType.DMA((2 * cols,)),
            pltpu.SemaphoreType.DMA((2 * cols,)),
        ],
        compiler_params=pltpu.CompilerParams(collective_id=1, has_side_effects=True),
    )(blocks, gram)


def gather_kernel(rows, piece_ref, out_ref, sends, receipts):
    here_row = lax.axis_index("row")
    here_col = lax.axis_index("col")
    peers = [(lax.rem(here_row + shift, rows), here_col) for shift in range(1, rows)]
    barrier = pltpu.get_barrier_semaphore()
    for peer in peers:
        pl.semaphore_signal(barrier, inc=1, device_id=peer, device_id_type=MESH)
    pl.semaphore_wait(barrier, len(peers))
    copies = []
    for number, peer in enumerate(peers):
        copy = pltpu.make_async_remote_copy(
            src_ref=piece_ref,
            dst_ref=out_ref.at[here_row],
            send_sem=sends.at[number],
            recv_sem=receipts.at[number],
            device_id=peer,
            device_id_type=MESH,
        )
        copy.start()
        copies.append(copy)
    out_ref[here_row] = piece_ref[...]
    for copy in copies:
        copy.wait()


def row_gather(piece):
    rows = lax.axis_size("row")
    flipped = piece.T.astype(jnp.float32)
    gathered = pl.pallas_call(
        functools.partial(gather_kernel, rows),
        out_shape=jax.ShapeDtypeStruct((rows,) + flipped.shape, jnp.float32),
        in_specs=[pl.BlockSpec(memory_space=pltpu.VMEM)],
        out_specs=pl.BlockSpec(memory_space=pltpu.VMEM),
        scratch_shapes=[
            pltpu.SemaphoreType.DMA((rows,)),
            pltpu.SemaphoreType.DMA((rows,)),
        ],
        compiler_params=pltpu.CompilerParams(collective_id=2, has_side_effects=True),
    )(flipped)
    return gathered.reshape(-1, flipped.shape[1]).T.astype(piece.dtype)


def body(
    multispectral, hyperspectral, row_start, col_factor, band_factor, response, blur_taps, offsets
):
    low_reach = (W + DEC - 1) // DEC
    columns = row_gather(col_factor)
    column_wide = extended(columns, (("col", 0),), W)
    column_down = down_matrix(blur_taps, offsets, columns.shape[0] // DEC, column_wide.shape[0])
    coarse_columns = apply_band(column_down, column_wide)
    merged = jnp.dot(response, band_factor, precision=FULL_PRECISION)
    multi_pairs = (merged[:, None, :] * columns.astype(jnp.float32)[None, :, :]).astype(
        jnp.bfloat16
    )
    hyper_pairs = (band_factor[:, None, :] * coarse_columns[None, :, :]).astype(jnp.bfloat16)
    multi_part = jnp.einsum(
        "kij,kjr->ir", multispectral, multi_pairs, preferred_element_type=jnp.float32
    )
    hyper_part = jnp.einsum(
        "kij,kjr->ir", hyperspectral, hyper_pairs, preferred_element_type=jnp.float32
    )
    column_part = jnp.einsum("jr,js->rs", columns, columns, preferred_element_type=jnp.float32)
    coarse_part = jnp.einsum("jr,js->rs", coarse_columns, coarse_columns, precision=FULL_PRECISION)
    cols = lax.axis_size("col")
    multi_blocks = multi_part.reshape(cols, -1, multi_part.shape[1])
    hyper_blocks = hyper_part.reshape(cols, -1, hyper_part.shape[1])
    joined = jnp.concatenate([multi_blocks, hyper_blocks], axis=1)
    joined, gram_sums = col_scatter(joined, jnp.concatenate([column_part, coarse_part], axis=0))
    column_gram = gram_sums[: column_part.shape[0]]
    coarse_gram = gram_sums[column_part.shape[0] :]
    band_gram = jnp.dot(band_factor.T, band_factor, precision=FULL_PRECISION)
    merged_gram = jnp.dot(merged.T, merged, precision=FULL_PRECISION)
    hyper_gram = coarse_gram * band_gram
    multi_gram = column_gram * merged_gram
    multi_sums = joined[: multi_blocks.shape[1]]
    hyper_sums = joined[multi_blocks.shape[1] :]
    start_rows = row_start
    grid = ("row", "col")

    fine_rows = start_rows.shape[0]
    fine_reach = W + DEC * low_reach
    halo = (ITERS + 1) * fine_reach
    coarse_halo = halo // DEC + low_reach
    wide_rows = fine_rows + 2 * halo
    count = lax.axis_size("row") * cols
    pieces = (start_rows, multi_sums, hyper_sums)
    reaches = (halo, halo, coarse_halo)
    tails = jnp.concatenate([piece[piece.shape[0] - reach :] for piece, reach in zip(pieces, reaches)])
    heads = jnp.concatenate([piece[:reach] for piece, reach in zip(pieces, reaches)])
    before = lax.ppermute(tails, grid, [(i, (i + 1) % count) for i in range(count)])
    after = lax.ppermute(heads, grid, [((i + 1) % count, i) for i in range(count)])
    wide = []
    corner = 0
    for piece, reach in zip(pieces, reaches):
        wide.append(
            jnp.concatenate(
                [before[corner : corner + reach], piece, after[corner : corner + reach]]
            )
        )
        corner += reach
    start_wide, multi_wide, hyper_wide = wide

    lifting = up_matrix(blur_taps, offsets, wide_rows // DEC + 2 * low_reach, low_reach)
    lowering = down_matrix(
        blur_taps, offsets, wide_rows // DEC + 2 * low_reach, wide_rows + 2 * fine_reach
    )
    blurring = jnp.dot(lifting, lowering, precision=FULL_PRECISION)
    blurring = blurring[:, fine_reach : fine_reach + wide_rows]

    def operate(values):
        restored = apply_band(blurring, values)
        return (
            jnp.dot(restored, hyper_gram, precision=FULL_PRECISION)
            + jnp.dot(values, multi_gram, precision=FULL_PRECISION)
            + RIDGE_TERM * values
        )

    def own(values):
        return values[halo : halo + fine_rows]

    def inner_sum(first_field, second_field):
        return grid_totals([jnp.sum(own(first_field) * own(second_field))])[0]

    right_side = apply_band(lifting, hyper_wide) + multi_wide
    solution = start_wide
    residual = right_side - operate(solution)
    direction = residual
    norm_now = None
    for iteration in range(ITERS):
        mapped = operate(direction)
        if norm_now is None:
            norm_now, curvature = grid_totals(
                [jnp.sum(own(residual) * own(residual)), jnp.sum(own(direction) * own(mapped))]
            )
        else:
            curvature = inner_sum(direction, mapped)
        step_size = norm_now / curvature
        solution = solution + step_size * direction
        residual = residual - step_size * mapped
        norm_next = inner_sum(residual, residual)
        direction = residual + norm_next / norm_now * direction
        norm_now = norm_next
    solution = own(solution)
    residual = own(residual)
    return (solution, residual)


def solution(mesh):
    in_specs = (
        P(None, "row", "col"),
        P(None, "row", "col"),
        P(("row", "col"), None),
        P("col", "row"),
        P(),
        P(),
        P(),
        P(),
    )
    out_specs = (P(("row", "col"), None), P(("row", "col"), None))
    return jax.shard_map(body, mesh=mesh, in_specs=in_specs, out_specs=out_specs, check_vma=False)
```

```python
import functools

import jax
import jax.numpy as jnp
from jax import lax
from jax.experimental import pallas as pl
from jax.experimental.pallas import tpu as pltpu
from jax.sharding import PartitionSpec as P

MESH = pl.DeviceIdType.MESH

DEC = 4
W = 8
ITERS = 4


RIDGE_TERM = 0.1
FULL_PRECISION = lax.Precision.HIGHEST


def extended(cells, sides, width):
    for axis, dim in sides:
        names = axis if isinstance(axis, tuple) else (axis,)
        count = 1
        for name in names:
            count *= lax.axis_size(name)
        head = lax.slice_in_dim(cells, 0, width, axis=dim)
        tail = lax.slice_in_dim(cells, cells.shape[dim] - width, cells.shape[dim], axis=dim)
        cells = jnp.concatenate(
            [
                lax.ppermute(tail, axis, [(i, (i + 1) % count) for i in range(count)]),
                cells,
                lax.ppermute(head, axis, [((i + 1) % count, i) for i in range(count)]),
            ],
            axis=dim,
        )
    return cells


def down_matrix(weights, offsets, rows_out, rows_in):
    outer = lax.broadcasted_iota(jnp.int32, (rows_out, rows_in, 1), 0)
    inner = lax.broadcasted_iota(jnp.int32, (rows_out, rows_in, 1), 1)
    hits = inner == DEC * outer + offsets[None, None, :] + W
    return jnp.sum(jnp.where(hits, weights[None, None, :], jnp.float32(0.0)), axis=2)


def up_matrix(weights, offsets, rows_in, low_margin):
    rows_out = (rows_in - 2 * low_margin) * DEC
    outer = lax.broadcasted_iota(jnp.int32, (rows_out, rows_in, 1), 0)
    inner = lax.broadcasted_iota(jnp.int32, (rows_out, rows_in, 1), 1)
    hits = DEC * inner == outer + DEC * low_margin - offsets[None, None, :]
    return jnp.sum(jnp.where(hits, weights[None, None, :], jnp.float32(0.0)), axis=2)


def apply_band(matrix, values):
    return jnp.dot(matrix, values.astype(jnp.float32), precision=FULL_PRECISION)


def total_kernel(rows, cols, part_ref, out_ref, col_held, row_held, sends, receipts):
    here_row = lax.axis_index("row")
    here_col = lax.axis_index("col")
    col_peers = [(here_row, lax.rem(here_col + shift, cols)) for shift in range(1, cols)]
    row_peers = [(lax.rem(here_row + shift, rows), here_col) for shift in range(1, rows)]
    barrier = pltpu.get_barrier_semaphore()
    for peer in col_peers + row_peers:
        pl.semaphore_signal(barrier, inc=1, device_id=peer, device_id_type=MESH)
    pl.semaphore_wait(barrier, len(col_peers) + len(row_peers))
    copies = []
    for number, peer in enumerate(col_peers):
        copy = pltpu.make_async_remote_copy(
            src_ref=part_ref,
            dst_ref=col_held.at[here_col],
            send_sem=sends.at[number],
            recv_sem=receipts.at[number],
            device_id=peer,
            device_id_type=MESH,
        )
        copy.start()
        copies.append(copy)
    col_held[here_col] = part_ref[...]
    for copy in copies:
        copy.wait()
    col_total = col_held[0]
    for source in range(1, cols):
        col_total = col_total + col_held[source]
    row_held[here_row] = col_total
    copies = []
    for number, peer in enumerate(row_peers):
        copy = pltpu.make_async_remote_copy(
            src_ref=row_held.at[here_row],
            dst_ref=row_held.at[here_row],
            send_sem=sends.at[cols + number],
            recv_sem=receipts.at[cols + number],
            device_id=peer,
            device_id_type=MESH,
        )
        copy.start()
        copies.append(copy)
    for copy in copies:
        copy.wait()
    total = row_held[0]
    for source in range(1, rows):
        total = total + row_held[source]
    out_ref[...] = total


def grid_totals(parts):
    rows = lax.axis_size("row")
    cols = lax.axis_size("col")
    lanes = jnp.pad(jnp.stack(parts), (0, 128 - len(parts)))
    tile = jnp.broadcast_to(lanes[None, :], (8, 128))
    summed = pl.pallas_call(
        functools.partial(total_kernel, rows, cols),
        out_shape=jax.ShapeDtypeStruct((8, 128), jnp.float32),
        in_specs=[pl.BlockSpec(memory_space=pltpu.VMEM)],
        out_specs=pl.BlockSpec(memory_space=pltpu.VMEM),
        scratch_shapes=[
            pltpu.VMEM((cols, 8, 128), jnp.float32),
            pltpu.VMEM((rows, 8, 128), jnp.float32),
            pltpu.SemaphoreType.DMA((rows + cols,)),
            pltpu.SemaphoreType.DMA((rows + cols,)),
        ],
        compiler_params=pltpu.CompilerParams(collective_id=0, has_side_effects=True),
    )(tile)
    return [summed[0, number] for number in range(len(parts))]


def scatter_kernel(cols, blocks_ref, gram_ref, sums_ref, grams_ref, held, gram_held, sends, receipts):
    here_row = lax.axis_index("row")
    here_col = lax.axis_index("col")
    peers = [lax.rem(here_col + shift, cols) for shift in range(1, cols)]
    barrier = pltpu.get_barrier_semaphore()
    for peer in peers:
        pl.semaphore_signal(barrier, inc=1, device_id=(here_row, peer), device_id_type=MESH)
    pl.semaphore_wait(barrier, len(peers))
    copies = []
    for number, peer in enumerate(peers):
        for slot, (source, target) in enumerate(
            ((blocks_ref.at[peer], held.at[here_col]), (gram_ref, gram_held.at[here_col]))
        ):
            copy = pltpu.make_async_remote_copy(
                src_ref=source,
                dst_ref=target,
                send_sem=sends.at[2 * number + slot],
                recv_sem=receipts.at[2 * number + slot],
                device_id=(here_row, peer),
                device_id_type=MESH,
            )
            copy.start()
            copies.append(copy)
    held[here_col] = blocks_ref[here_col]
    gram_held[here_col] = gram_ref[...]
    for copy in copies:
        copy.wait()
    sums = held[0]
    grams = gram_held[0]
    for source in range(1, cols):
        sums = sums + held[source]
        grams = grams + gram_held[source]
    sums_ref[...] = sums
    grams_ref[...] = grams


def col_scatter(blocks, gram):
    cols = blocks.shape[0]
    return pl.pallas_call(
        functools.partial(scatter_kernel, cols),
        out_shape=(
            jax.ShapeDtypeStruct(blocks.shape[1:], jnp.float32),
            jax.ShapeDtypeStruct(gram.shape, jnp.float32),
        ),
        in_specs=[pl.BlockSpec(memory_space=pltpu.VMEM)] * 2,
        out_specs=(pl.BlockSpec(memory_space=pltpu.VMEM),) * 2,
        scratch_shapes=[
            pltpu.VMEM(blocks.shape, jnp.float32),
            pltpu.VMEM((cols,) + gram.shape, jnp.float32),
            pltpu.SemaphoreType.DMA((2 * cols,)),
            pltpu.SemaphoreType.DMA((2 * cols,)),
        ],
        compiler_params=pltpu.CompilerParams(collective_id=1, has_side_effects=True),
    )(blocks, gram)


def gather_kernel(rows, piece_ref, out_ref, sends, receipts):
    here_row = lax.axis_index("row")
    here_col = lax.axis_index("col")
    peers = [(lax.rem(here_row + shift, rows), here_col) for shift in range(1, rows)]
    barrier = pltpu.get_barrier_semaphore()
    for peer in peers:
        pl.semaphore_signal(barrier, inc=1, device_id=peer, device_id_type=MESH)
    pl.semaphore_wait(barrier, len(peers))
    copies = []
    for number, peer in enumerate(peers):
        copy = pltpu.make_async_remote_copy(
            src_ref=piece_ref,
            dst_ref=out_ref.at[here_row],
            send_sem=sends.at[number],
            recv_sem=receipts.at[number],
            device_id=peer,
            device_id_type=MESH,
        )
        copy.start()
        copies.append(copy)
    out_ref[here_row] = piece_ref[...]
    for copy in copies:
        copy.wait()


def row_gather(piece):
    rows = lax.axis_size("row")
    flipped = piece.T.astype(jnp.float32)
    gathered = pl.pallas_call(
        functools.partial(gather_kernel, rows),
        out_shape=jax.ShapeDtypeStruct((rows,) + flipped.shape, jnp.float32),
        in_specs=[pl.BlockSpec(memory_space=pltpu.VMEM)],
        out_specs=pl.BlockSpec(memory_space=pltpu.VMEM),
        scratch_shapes=[
            pltpu.SemaphoreType.DMA((rows,)),
            pltpu.SemaphoreType.DMA((rows,)),
        ],
        compiler_params=pltpu.CompilerParams(collective_id=2, has_side_effects=True),
    )(flipped)
    return gathered.reshape(-1, flipped.shape[1]).T.astype(piece.dtype)


def body(
    multispectral, hyperspectral, row_start, col_factor, band_factor, response, blur_taps, offsets
):
    low_reach = (W + DEC - 1) // DEC
    columns = row_gather(col_factor)
    column_wide = extended(columns, (("col", 0),), W)
    column_down = down_matrix(blur_taps, offsets, columns.shape[0] // DEC, column_wide.shape[0])
    coarse_columns = apply_band(column_down, column_wide)
    merged = jnp.dot(response, band_factor, precision=FULL_PRECISION)
    multi_pairs = (merged[:, None, :] * columns.astype(jnp.float32)[None, :, :]).astype(
        jnp.bfloat16
    )
    hyper_pairs = (band_factor[:, None, :] * coarse_columns[None, :, :]).astype(jnp.bfloat16)
    multi_part = jnp.einsum(
        "kij,kjr->ir", multispectral, multi_pairs, preferred_element_type=jnp.float32
    )
    hyper_part = jnp.einsum(
        "kij,kjr->ir", hyperspectral, hyper_pairs, preferred_element_type=jnp.float32
    )
    column_part = jnp.einsum("jr,js->rs", columns, columns, preferred_element_type=jnp.float32)
    coarse_part = jnp.einsum("jr,js->rs", coarse_columns, coarse_columns, precision=FULL_PRECISION)
    cols = lax.axis_size("col")
    multi_blocks = multi_part.reshape(cols, -1, multi_part.shape[1])
    hyper_blocks = hyper_part.reshape(cols, -1, hyper_part.shape[1])
    joined = jnp.concatenate([multi_blocks, hyper_blocks], axis=1)
    joined, gram_sums = col_scatter(joined, jnp.concatenate([column_part, coarse_part], axis=0))
    column_gram = gram_sums[: column_part.shape[0]]
    coarse_gram = gram_sums[column_part.shape[0] :]
    band_gram = jnp.dot(band_factor.T, band_factor, precision=FULL_PRECISION)
    merged_gram = jnp.dot(merged.T, merged, precision=FULL_PRECISION)
    hyper_gram = coarse_gram * band_gram
    multi_gram = column_gram * merged_gram
    multi_sums = joined[: multi_blocks.shape[1]]
    hyper_sums = joined[multi_blocks.shape[1] :]
    start_rows = row_start
    grid = ("row", "col")

    fine_rows = start_rows.shape[0]
    fine_reach = W + DEC * low_reach
    halo = (ITERS + 1) * fine_reach
    coarse_halo = halo // DEC + low_reach
    wide_rows = fine_rows + 2 * halo
    count = lax.axis_size("row") * cols
    pieces = (start_rows, multi_sums, hyper_sums)
    reaches = (halo, halo, coarse_halo)
    tails = jnp.concatenate([piece[piece.shape[0] - reach :] for piece, reach in zip(pieces, reaches)])
    heads = jnp.concatenate([piece[:reach] for piece, reach in zip(pieces, reaches)])
    before = lax.ppermute(tails, grid, [(i, (i + 1) % count) for i in range(count)])
    after = lax.ppermute(heads, grid, [((i + 1) % count, i) for i in range(count)])
    wide = []
    corner = 0
    for piece, reach in zip(pieces, reaches):
        wide.append(
            jnp.concatenate(
                [before[corner : corner + reach], piece, after[corner : corner + reach]]
            )
        )
        corner += reach
    start_wide, multi_wide, hyper_wide = wide

    lifting = up_matrix(blur_taps, offsets, wide_rows // DEC + 2 * low_reach, low_reach)
    lowering = down_matrix(
        blur_taps, offsets, wide_rows // DEC + 2 * low_reach, wide_rows + 2 * fine_reach
    )
    blurring = jnp.dot(lifting, lowering, precision=FULL_PRECISION)
    blurring = blurring[:, fine_reach : fine_reach + wide_rows]

    def operate(values):
        restored = apply_band(blurring, values)
        return (
            jnp.dot(restored, hyper_gram, precision=FULL_PRECISION)
            + jnp.dot(values, multi_gram, precision=FULL_PRECISION)
            + RIDGE_TERM * values
        )

    def own(values):
        return values[halo : halo + fine_rows]

    right_side = apply_band(lifting, hyper_wide) + multi_wide
    solution = start_wide
    residual = right_side - operate(solution)
    direction = residual
    norm_now = None
    for iteration in range(ITERS):
        mapped = operate(direction)
        parts = [
            jnp.sum(own(direction) * own(mapped)),
            jnp.sum(own(residual) * own(mapped)),
            jnp.sum(own(mapped) * own(mapped)),
        ]
        if norm_now is None:
            parts.append(jnp.sum(own(residual) * own(residual)))
            curvature, cross, power, norm_now = grid_totals(parts)
        else:
            curvature, cross, power = grid_totals(parts)
        step_size = norm_now / curvature
        solution = solution + step_size * direction
        residual = residual - step_size * mapped
        norm_next = norm_now - 2 * step_size * cross + step_size * step_size * power
        direction = residual + norm_next / norm_now * direction
        norm_now = norm_next
    solution = own(solution)
    residual = own(residual)
    return (solution, residual)


def solution(mesh):
    in_specs = (
        P(None, "row", "col"),
        P(None, "row", "col"),
        P(("row", "col"), None),
        P("col", "row"),
        P(),
        P(),
        P(),
        P(),
    )
    out_specs = (P(("row", "col"), None), P(("row", "col"), None))
    return jax.shard_map(body, mesh=mesh, in_specs=in_specs, out_specs=out_specs, check_vma=False)
```

```python
import functools

import jax
import jax.numpy as jnp
from jax import lax
from jax.experimental import pallas as pl
from jax.experimental.pallas import tpu as pltpu
from jax.sharding import PartitionSpec as P

MESH = pl.DeviceIdType.MESH

DEC = 4
W = 8
ITERS = 4


RIDGE_TERM = 0.1
FULL_PRECISION = lax.Precision.HIGHEST


def extended(cells, sides, width):
    for axis, dim in sides:
        names = axis if isinstance(axis, tuple) else (axis,)
        count = 1
        for name in names:
            count *= lax.axis_size(name)
        head = lax.slice_in_dim(cells, 0, width, axis=dim)
        tail = lax.slice_in_dim(cells, cells.shape[dim] - width, cells.shape[dim], axis=dim)
        cells = jnp.concatenate(
            [
                lax.ppermute(tail, axis, [(i, (i + 1) % count) for i in range(count)]),
                cells,
                lax.ppermute(head, axis, [((i + 1) % count, i) for i in range(count)]),
            ],
            axis=dim,
        )
    return cells


def down_matrix(weights, offsets, rows_out, rows_in):
    outer = lax.broadcasted_iota(jnp.int32, (rows_out, rows_in, 1), 0)
    inner = lax.broadcasted_iota(jnp.int32, (rows_out, rows_in, 1), 1)
    hits = inner == DEC * outer + offsets[None, None, :] + W
    return jnp.sum(jnp.where(hits, weights[None, None, :], jnp.float32(0.0)), axis=2)


def up_matrix(weights, offsets, rows_in, low_margin):
    rows_out = (rows_in - 2 * low_margin) * DEC
    outer = lax.broadcasted_iota(jnp.int32, (rows_out, rows_in, 1), 0)
    inner = lax.broadcasted_iota(jnp.int32, (rows_out, rows_in, 1), 1)
    hits = DEC * inner == outer + DEC * low_margin - offsets[None, None, :]
    return jnp.sum(jnp.where(hits, weights[None, None, :], jnp.float32(0.0)), axis=2)


def apply_band(matrix, values):
    return jnp.dot(matrix, values.astype(jnp.float32), precision=FULL_PRECISION)


def total_kernel(rows, cols, part_ref, out_ref, col_held, row_held, sends, receipts):
    here_row = lax.axis_index("row")
    here_col = lax.axis_index("col")
    col_peers = [(here_row, lax.rem(here_col + shift, cols)) for shift in range(1, cols)]
    row_peers = [(lax.rem(here_row + shift, rows), here_col) for shift in range(1, rows)]
    barrier = pltpu.get_barrier_semaphore()
    for peer in col_peers + row_peers:
        pl.semaphore_signal(barrier, inc=1, device_id=peer, device_id_type=MESH)
    pl.semaphore_wait(barrier, len(col_peers) + len(row_peers))
    copies = []
    for number, peer in enumerate(col_peers):
        copy = pltpu.make_async_remote_copy(
            src_ref=part_ref,
            dst_ref=col_held.at[here_col],
            send_sem=sends.at[number],
            recv_sem=receipts.at[number],
            device_id=peer,
            device_id_type=MESH,
        )
        copy.start()
        copies.append(copy)
    col_held[here_col] = part_ref[...]
    for copy in copies:
        copy.wait()
    col_total = col_held[0]
    for source in range(1, cols):
        col_total = col_total + col_held[source]
    row_held[here_row] = col_total
    copies = []
    for number, peer in enumerate(row_peers):
        copy = pltpu.make_async_remote_copy(
            src_ref=row_held.at[here_row],
            dst_ref=row_held.at[here_row],
            send_sem=sends.at[cols + number],
            recv_sem=receipts.at[cols + number],
            device_id=peer,
            device_id_type=MESH,
        )
        copy.start()
        copies.append(copy)
    for copy in copies:
        copy.wait()
    total = row_held[0]
    for source in range(1, rows):
        total = total + row_held[source]
    out_ref[...] = total


def grid_totals(parts):
    rows = lax.axis_size("row")
    cols = lax.axis_size("col")
    lanes = jnp.pad(jnp.stack(parts), (0, 128 - len(parts)))
    tile = jnp.broadcast_to(lanes[None, :], (8, 128))
    summed = pl.pallas_call(
        functools.partial(total_kernel, rows, cols),
        out_shape=jax.ShapeDtypeStruct((8, 128), jnp.float32),
        in_specs=[pl.BlockSpec(memory_space=pltpu.VMEM)],
        out_specs=pl.BlockSpec(memory_space=pltpu.VMEM),
        scratch_shapes=[
            pltpu.VMEM((cols, 8, 128), jnp.float32),
            pltpu.VMEM((rows, 8, 128), jnp.float32),
            pltpu.SemaphoreType.DMA((rows + cols,)),
            pltpu.SemaphoreType.DMA((rows + cols,)),
        ],
        compiler_params=pltpu.CompilerParams(collective_id=0, has_side_effects=True),
    )(tile)
    return [summed[0, number] for number in range(len(parts))]


def scatter_kernel(cols, blocks_ref, gram_ref, sums_ref, grams_ref, held, gram_held, sends, receipts):
    here_row = lax.axis_index("row")
    here_col = lax.axis_index("col")
    peers = [lax.rem(here_col + shift, cols) for shift in range(1, cols)]
    barrier = pltpu.get_barrier_semaphore()
    for peer in peers:
        pl.semaphore_signal(barrier, inc=1, device_id=(here_row, peer), device_id_type=MESH)
    pl.semaphore_wait(barrier, len(peers))
    copies = []
    for number, peer in enumerate(peers):
        for slot, (source, target) in enumerate(
            ((blocks_ref.at[peer], held.at[here_col]), (gram_ref.at[peer], gram_held.at[here_col]))
        ):
            copy = pltpu.make_async_remote_copy(
                src_ref=source,
                dst_ref=target,
                send_sem=sends.at[2 * number + slot],
                recv_sem=receipts.at[2 * number + slot],
                device_id=(here_row, peer),
                device_id_type=MESH,
            )
            copy.start()
            copies.append(copy)
    held[here_col] = blocks_ref[here_col]
    gram_held[here_col] = gram_ref[here_col]
    for copy in copies:
        copy.wait()
    sums = held[0]
    grams = gram_held[0]
    for source in range(1, cols):
        sums = sums + held[source]
        grams = grams + gram_held[source]
    sums_ref[...] = sums
    grams_ref[here_col] = grams
    copies = []
    for number, peer in enumerate(peers):
        copy = pltpu.make_async_remote_copy(
            src_ref=grams_ref.at[here_col],
            dst_ref=grams_ref.at[here_col],
            send_sem=sends.at[2 * cols + number],
            recv_sem=receipts.at[2 * cols + number],
            device_id=(here_row, peer),
            device_id_type=MESH,
        )
        copy.start()
        copies.append(copy)
    for copy in copies:
        copy.wait()


def col_scatter(blocks, gram):
    cols = blocks.shape[0]
    gram_blocks = gram.reshape(cols, -1, gram.shape[1])
    sums, grams = pl.pallas_call(
        functools.partial(scatter_kernel, cols),
        out_shape=(
            jax.ShapeDtypeStruct(blocks.shape[1:], jnp.float32),
            jax.ShapeDtypeStruct(gram_blocks.shape, jnp.float32),
        ),
        in_specs=[pl.BlockSpec(memory_space=pltpu.VMEM)] * 2,
        out_specs=(pl.BlockSpec(memory_space=pltpu.VMEM),) * 2,
        scratch_shapes=[
            pltpu.VMEM(blocks.shape, jnp.float32),
            pltpu.VMEM(gram_blocks.shape, jnp.float32),
            pltpu.SemaphoreType.DMA((3 * cols,)),
            pltpu.SemaphoreType.DMA((3 * cols,)),
        ],
        compiler_params=pltpu.CompilerParams(collective_id=1, has_side_effects=True),
    )(blocks, gram_blocks)
    return sums, grams.reshape(gram.shape)


def gather_kernel(rows, piece_ref, out_ref, sends, receipts):
    here_row = lax.axis_index("row")
    here_col = lax.axis_index("col")
    peers = [(lax.rem(here_row + shift, rows), here_col) for shift in range(1, rows)]
    barrier = pltpu.get_barrier_semaphore()
    for peer in peers:
        pl.semaphore_signal(barrier, inc=1, device_id=peer, device_id_type=MESH)
    pl.semaphore_wait(barrier, len(peers))
    copies = []
    for number, peer in enumerate(peers):
        copy = pltpu.make_async_remote_copy(
            src_ref=piece_ref,
            dst_ref=out_ref.at[here_row],
            send_sem=sends.at[number],
            recv_sem=receipts.at[number],
            device_id=peer,
            device_id_type=MESH,
        )
        copy.start()
        copies.append(copy)
    out_ref[here_row] = piece_ref[...]
    for copy in copies:
        copy.wait()


def row_gather(piece):
    rows = lax.axis_size("row")
    flipped = piece.T.astype(jnp.float32)
    gathered = pl.pallas_call(
        functools.partial(gather_kernel, rows),
        out_shape=jax.ShapeDtypeStruct((rows,) + flipped.shape, jnp.float32),
        in_specs=[pl.BlockSpec(memory_space=pltpu.VMEM)],
        out_specs=pl.BlockSpec(memory_space=pltpu.VMEM),
        scratch_shapes=[
            pltpu.SemaphoreType.DMA((rows,)),
            pltpu.SemaphoreType.DMA((rows,)),
        ],
        compiler_params=pltpu.CompilerParams(collective_id=2, has_side_effects=True),
    )(flipped)
    return gathered.reshape(-1, flipped.shape[1]).T.astype(piece.dtype)


def body(
    multispectral, hyperspectral, row_start, col_factor, band_factor, response, blur_taps, offsets
):
    low_reach = (W + DEC - 1) // DEC
    columns = row_gather(col_factor)
    column_wide = extended(columns, (("col", 0),), W)
    column_down = down_matrix(blur_taps, offsets, columns.shape[0] // DEC, column_wide.shape[0])
    coarse_columns = apply_band(column_down, column_wide)
    merged = jnp.dot(response, band_factor, precision=FULL_PRECISION)
    multi_pairs = (merged[:, None, :] * columns.astype(jnp.float32)[None, :, :]).astype(
        jnp.bfloat16
    )
    hyper_pairs = (band_factor[:, None, :] * coarse_columns[None, :, :]).astype(jnp.bfloat16)
    multi_part = jnp.einsum(
        "kij,kjr->ir", multispectral, multi_pairs, preferred_element_type=jnp.float32
    )
    hyper_part = jnp.einsum(
        "kij,kjr->ir", hyperspectral, hyper_pairs, preferred_element_type=jnp.float32
    )
    column_part = jnp.einsum("jr,js->rs", columns, columns, preferred_element_type=jnp.float32)
    coarse_part = jnp.einsum("jr,js->rs", coarse_columns, coarse_columns, precision=FULL_PRECISION)
    cols = lax.axis_size("col")
    multi_blocks = multi_part.reshape(cols, -1, multi_part.shape[1])
    hyper_blocks = hyper_part.reshape(cols, -1, hyper_part.shape[1])
    joined = jnp.concatenate([multi_blocks, hyper_blocks], axis=1)
    joined, gram_sums = col_scatter(joined, jnp.concatenate([column_part, coarse_part], axis=0))
    column_gram = gram_sums[: column_part.shape[0]]
    coarse_gram = gram_sums[column_part.shape[0] :]
    band_gram = jnp.dot(band_factor.T, band_factor, precision=FULL_PRECISION)
    merged_gram = jnp.dot(merged.T, merged, precision=FULL_PRECISION)
    hyper_gram = coarse_gram * band_gram
    multi_gram = column_gram * merged_gram
    multi_sums = joined[: multi_blocks.shape[1]]
    hyper_sums = joined[multi_blocks.shape[1] :]
    start_rows = row_start
    grid = ("row", "col")

    fine_rows = start_rows.shape[0]
    fine_reach = W + DEC * low_reach
    halo = (ITERS + 1) * fine_reach
    coarse_halo = halo // DEC + low_reach
    wide_rows = fine_rows + 2 * halo
    count = lax.axis_size("row") * cols
    pieces = (start_rows, multi_sums, hyper_sums)
    reaches = (halo, halo, coarse_halo)
    tails = jnp.concatenate([piece[piece.shape[0] - reach :] for piece, reach in zip(pieces, reaches)])
    heads = jnp.concatenate([piece[:reach] for piece, reach in zip(pieces, reaches)])
    before = lax.ppermute(tails, grid, [(i, (i + 1) % count) for i in range(count)])
    after = lax.ppermute(heads, grid, [((i + 1) % count, i) for i in range(count)])
    wide = []
    corner = 0
    for piece, reach in zip(pieces, reaches):
        wide.append(
            jnp.concatenate(
                [before[corner : corner + reach], piece, after[corner : corner + reach]]
            )
        )
        corner += reach
    start_wide, multi_wide, hyper_wide = wide

    lifting = up_matrix(blur_taps, offsets, wide_rows // DEC + 2 * low_reach, low_reach)
    lowering = down_matrix(
        blur_taps, offsets, wide_rows // DEC + 2 * low_reach, wide_rows + 2 * fine_reach
    )
    blurring = jnp.dot(lifting, lowering, precision=FULL_PRECISION)
    blurring = blurring[:, fine_reach : fine_reach + wide_rows]

    def operate(values):
        restored = apply_band(blurring, values)
        return (
            jnp.dot(restored, hyper_gram, precision=FULL_PRECISION)
            + jnp.dot(values, multi_gram, precision=FULL_PRECISION)
            + RIDGE_TERM * values
        )

    def own(values):
        return values[halo : halo + fine_rows]

    right_side = apply_band(lifting, hyper_wide) + multi_wide
    solution = start_wide
    residual = right_side - operate(solution)
    direction = residual
    norm_now = None
    for iteration in range(ITERS):
        mapped = operate(direction)
        parts = [
            jnp.sum(own(direction) * own(mapped)),
            jnp.sum(own(residual) * own(mapped)),
            jnp.sum(own(mapped) * own(mapped)),
        ]
        if norm_now is None:
            parts.append(jnp.sum(own(residual) * own(residual)))
            curvature, cross, power, norm_now = grid_totals(parts)
        else:
            curvature, cross, power = grid_totals(parts)
        step_size = norm_now / curvature
        solution = solution + step_size * direction
        residual = residual - step_size * mapped
        norm_next = norm_now - 2 * step_size * cross + step_size * step_size * power
        direction = residual + norm_next / norm_now * direction
        norm_now = norm_next
    solution = own(solution)
    residual = own(residual)
    return (solution, residual)


def solution(mesh):
    in_specs = (
        P(None, "row", "col"),
        P(None, "row", "col"),
        P(("row", "col"), None),
        P("col", "row"),
        P(),
        P(),
        P(),
        P(),
    )
    out_specs = (P(("row", "col"), None), P(("row", "col"), None))
    return jax.shard_map(body, mesh=mesh, in_specs=in_specs, out_specs=out_specs, check_vma=False)
```

```python
import functools

import jax
import jax.numpy as jnp
from jax import lax
from jax.experimental import pallas as pl
from jax.experimental.pallas import tpu as pltpu
from jax.sharding import PartitionSpec as P

MESH = pl.DeviceIdType.MESH

DEC = 4
W = 8
ITERS = 4


RIDGE_TERM = 0.1
FULL_PRECISION = lax.Precision.HIGHEST


def extended(cells, sides, width):
    for axis, dim in sides:
        names = axis if isinstance(axis, tuple) else (axis,)
        count = 1
        for name in names:
            count *= lax.axis_size(name)
        head = lax.slice_in_dim(cells, 0, width, axis=dim)
        tail = lax.slice_in_dim(cells, cells.shape[dim] - width, cells.shape[dim], axis=dim)
        cells = jnp.concatenate(
            [
                lax.ppermute(tail, axis, [(i, (i + 1) % count) for i in range(count)]),
                cells,
                lax.ppermute(head, axis, [((i + 1) % count, i) for i in range(count)]),
            ],
            axis=dim,
        )
    return cells


def down_matrix(weights, offsets, rows_out, rows_in):
    outer = lax.broadcasted_iota(jnp.int32, (rows_out, rows_in, 1), 0)
    inner = lax.broadcasted_iota(jnp.int32, (rows_out, rows_in, 1), 1)
    hits = inner == DEC * outer + offsets[None, None, :] + W
    return jnp.sum(jnp.where(hits, weights[None, None, :], jnp.float32(0.0)), axis=2)


def up_matrix(weights, offsets, rows_in, low_margin):
    rows_out = (rows_in - 2 * low_margin) * DEC
    outer = lax.broadcasted_iota(jnp.int32, (rows_out, rows_in, 1), 0)
    inner = lax.broadcasted_iota(jnp.int32, (rows_out, rows_in, 1), 1)
    hits = DEC * inner == outer + DEC * low_margin - offsets[None, None, :]
    return jnp.sum(jnp.where(hits, weights[None, None, :], jnp.float32(0.0)), axis=2)


def apply_band(matrix, values):
    return jnp.dot(matrix, values.astype(jnp.float32), precision=FULL_PRECISION)


def total_kernel(rows, cols, part_ref, out_ref, col_held, row_held, sends, receipts):
    here_row = lax.axis_index("row")
    here_col = lax.axis_index("col")
    col_peers = [(here_row, lax.rem(here_col + shift, cols)) for shift in range(1, cols)]
    row_peers = [(lax.rem(here_row + shift, rows), here_col) for shift in range(1, rows)]
    barrier = pltpu.get_barrier_semaphore()
    for peer in col_peers + row_peers:
        pl.semaphore_signal(barrier, inc=1, device_id=peer, device_id_type=MESH)
    pl.semaphore_wait(barrier, len(col_peers) + len(row_peers))
    copies = []
    for number, peer in enumerate(col_peers):
        copy = pltpu.make_async_remote_copy(
            src_ref=part_ref,
            dst_ref=col_held.at[here_col],
            send_sem=sends.at[number],
            recv_sem=receipts.at[number],
            device_id=peer,
            device_id_type=MESH,
        )
        copy.start()
        copies.append(copy)
    col_held[here_col] = part_ref[...]
    for copy in copies:
        copy.wait()
    col_total = col_held[0]
    for source in range(1, cols):
        col_total = col_total + col_held[source]
    row_held[here_row] = col_total
    copies = []
    for number, peer in enumerate(row_peers):
        copy = pltpu.make_async_remote_copy(
            src_ref=row_held.at[here_row],
            dst_ref=row_held.at[here_row],
            send_sem=sends.at[cols + number],
            recv_sem=receipts.at[cols + number],
            device_id=peer,
            device_id_type=MESH,
        )
        copy.start()
        copies.append(copy)
    for copy in copies:
        copy.wait()
    total = row_held[0]
    for source in range(1, rows):
        total = total + row_held[source]
    out_ref[...] = total


def grid_totals(parts):
    rows = lax.axis_size("row")
    cols = lax.axis_size("col")
    lanes = jnp.pad(jnp.stack(parts), (0, 128 - len(parts)))
    tile = jnp.broadcast_to(lanes[None, :], (8, 128))
    summed = pl.pallas_call(
        functools.partial(total_kernel, rows, cols),
        out_shape=jax.ShapeDtypeStruct((8, 128), jnp.float32),
        in_specs=[pl.BlockSpec(memory_space=pltpu.VMEM)],
        out_specs=pl.BlockSpec(memory_space=pltpu.VMEM),
        scratch_shapes=[
            pltpu.VMEM((cols, 8, 128), jnp.float32),
            pltpu.VMEM((rows, 8, 128), jnp.float32),
            pltpu.SemaphoreType.DMA((rows + cols,)),
            pltpu.SemaphoreType.DMA((rows + cols,)),
        ],
        compiler_params=pltpu.CompilerParams(collective_id=0, has_side_effects=True),
    )(tile)
    return [summed[0, number] for number in range(len(parts))]


def scatter_kernel(cols, blocks_ref, gram_ref, sums_ref, grams_ref, held, gram_held, sends, receipts):
    here_row = lax.axis_index("row")
    here_col = lax.axis_index("col")
    peers = [lax.rem(here_col + shift, cols) for shift in range(1, cols)]
    barrier = pltpu.get_barrier_semaphore()
    for peer in peers:
        pl.semaphore_signal(barrier, inc=1, device_id=(here_row, peer), device_id_type=MESH)
    pl.semaphore_wait(barrier, len(peers))
    copies = []
    for number, peer in enumerate(peers):
        for slot, (source, target) in enumerate(
            ((blocks_ref.at[peer], held.at[here_col]), (gram_ref.at[peer], gram_held.at[here_col]))
        ):
            copy = pltpu.make_async_remote_copy(
                src_ref=source,
                dst_ref=target,
                send_sem=sends.at[2 * number + slot],
                recv_sem=receipts.at[2 * number + slot],
                device_id=(here_row, peer),
                device_id_type=MESH,
            )
            copy.start()
            copies.append(copy)
    held[here_col] = blocks_ref[here_col]
    gram_held[here_col] = gram_ref[here_col]
    for copy in copies:
        copy.wait()
    sums = held[0]
    grams = gram_held[0]
    for source in range(1, cols):
        sums = sums + held[source]
        grams = grams + gram_held[source]
    sums_ref[...] = sums
    grams_ref[here_col] = grams
    copies = []
    for number, peer in enumerate(peers):
        copy = pltpu.make_async_remote_copy(
            src_ref=grams_ref.at[here_col],
            dst_ref=grams_ref.at[here_col],
            send_sem=sends.at[2 * cols + number],
            recv_sem=receipts.at[2 * cols + number],
            device_id=(here_row, peer),
            device_id_type=MESH,
        )
        copy.start()
        copies.append(copy)
    for copy in copies:
        copy.wait()


def col_scatter(blocks, gram):
    cols = blocks.shape[0]
    gram_blocks = gram.reshape(cols, -1, gram.shape[1])
    sums, grams = pl.pallas_call(
        functools.partial(scatter_kernel, cols),
        out_shape=(
            jax.ShapeDtypeStruct(blocks.shape[1:], jnp.float32),
            jax.ShapeDtypeStruct(gram_blocks.shape, jnp.float32),
        ),
        in_specs=[pl.BlockSpec(memory_space=pltpu.VMEM)] * 2,
        out_specs=(pl.BlockSpec(memory_space=pltpu.VMEM),) * 2,
        scratch_shapes=[
            pltpu.VMEM(blocks.shape, jnp.float32),
            pltpu.VMEM(gram_blocks.shape, jnp.float32),
            pltpu.SemaphoreType.DMA((3 * cols,)),
            pltpu.SemaphoreType.DMA((3 * cols,)),
        ],
        compiler_params=pltpu.CompilerParams(collective_id=1, has_side_effects=True),
    )(blocks, gram_blocks)
    return sums, grams.reshape(gram.shape)


def gather_kernel(rows, piece_ref, out_ref, sends, receipts):
    here_row = lax.axis_index("row")
    here_col = lax.axis_index("col")
    peers = [(lax.rem(here_row + shift, rows), here_col) for shift in range(1, rows)]
    barrier = pltpu.get_barrier_semaphore()
    for peer in peers:
        pl.semaphore_signal(barrier, inc=1, device_id=peer, device_id_type=MESH)
    pl.semaphore_wait(barrier, len(peers))
    copies = []
    for number, peer in enumerate(peers):
        copy = pltpu.make_async_remote_copy(
            src_ref=piece_ref,
            dst_ref=out_ref.at[here_row],
            send_sem=sends.at[number],
            recv_sem=receipts.at[number],
            device_id=peer,
            device_id_type=MESH,
        )
        copy.start()
        copies.append(copy)
    out_ref[here_row] = piece_ref[...]
    for copy in copies:
        copy.wait()


def row_gather(piece):
    rows = lax.axis_size("row")
    flipped = piece.T.astype(jnp.float32)
    gathered = pl.pallas_call(
        functools.partial(gather_kernel, rows),
        out_shape=jax.ShapeDtypeStruct((rows,) + flipped.shape, jnp.float32),
        in_specs=[pl.BlockSpec(memory_space=pltpu.VMEM)],
        out_specs=pl.BlockSpec(memory_space=pltpu.VMEM),
        scratch_shapes=[
            pltpu.SemaphoreType.DMA((rows,)),
            pltpu.SemaphoreType.DMA((rows,)),
        ],
        compiler_params=pltpu.CompilerParams(collective_id=2, has_side_effects=True),
    )(flipped)
    return gathered.reshape(-1, flipped.shape[1]).T.astype(piece.dtype)


def body(
    multispectral, hyperspectral, row_start, col_factor, band_factor, response, blur_taps, offsets
):
    low_reach = (W + DEC - 1) // DEC
    columns = row_gather(col_factor)
    column_wide = extended(columns, (("col", 0),), W)
    column_down = down_matrix(blur_taps, offsets, columns.shape[0] // DEC, column_wide.shape[0])
    coarse_columns = apply_band(column_down, column_wide)
    merged = jnp.dot(response, band_factor, precision=FULL_PRECISION)
    multi_pairs = (merged[:, None, :] * columns.astype(jnp.float32)[None, :, :]).astype(
        jnp.bfloat16
    )
    hyper_pairs = (band_factor[:, None, :] * coarse_columns[None, :, :]).astype(jnp.bfloat16)
    multi_part = jnp.dot(multispectral[0], multi_pairs[0], preferred_element_type=jnp.float32)
    for band in range(1, multispectral.shape[0]):
        multi_part = multi_part + jnp.dot(
            multispectral[band], multi_pairs[band], preferred_element_type=jnp.float32
        )
    hyper_part = jnp.einsum(
        "kij,kjr->ir", hyperspectral, hyper_pairs, preferred_element_type=jnp.float32
    )
    column_part = jnp.einsum("jr,js->rs", columns, columns, preferred_element_type=jnp.float32)
    coarse_part = jnp.einsum("jr,js->rs", coarse_columns, coarse_columns, precision=FULL_PRECISION)
    cols = lax.axis_size("col")
    multi_blocks = multi_part.reshape(cols, -1, multi_part.shape[1])
    hyper_blocks = hyper_part.reshape(cols, -1, hyper_part.shape[1])
    joined = jnp.concatenate([multi_blocks, hyper_blocks], axis=1)
    joined, gram_sums = col_scatter(joined, jnp.concatenate([column_part, coarse_part], axis=0))
    column_gram = gram_sums[: column_part.shape[0]]
    coarse_gram = gram_sums[column_part.shape[0] :]
    band_gram = jnp.dot(band_factor.T, band_factor, precision=FULL_PRECISION)
    merged_gram = jnp.dot(merged.T, merged, precision=FULL_PRECISION)
    hyper_gram = coarse_gram * band_gram
    multi_gram = column_gram * merged_gram
    multi_sums = joined[: multi_blocks.shape[1]]
    hyper_sums = joined[multi_blocks.shape[1] :]
    start_rows = row_start
    grid = ("row", "col")

    fine_rows = start_rows.shape[0]
    fine_reach = W + DEC * low_reach
    halo = (ITERS + 1) * fine_reach
    coarse_halo = halo // DEC + low_reach
    wide_rows = fine_rows + 2 * halo
    count = lax.axis_size("row") * cols
    pieces = (start_rows, multi_sums, hyper_sums)
    reaches = (halo, halo, coarse_halo)
    tails = jnp.concatenate([piece[piece.shape[0] - reach :] for piece, reach in zip(pieces, reaches)])
    heads = jnp.concatenate([piece[:reach] for piece, reach in zip(pieces, reaches)])
    before = lax.ppermute(tails, grid, [(i, (i + 1) % count) for i in range(count)])
    after = lax.ppermute(heads, grid, [((i + 1) % count, i) for i in range(count)])
    wide = []
    corner = 0
    for piece, reach in zip(pieces, reaches):
        wide.append(
            jnp.concatenate(
                [before[corner : corner + reach], piece, after[corner : corner + reach]]
            )
        )
        corner += reach
    start_wide, multi_wide, hyper_wide = wide

    lifting = up_matrix(blur_taps, offsets, wide_rows // DEC + 2 * low_reach, low_reach)
    lowering = down_matrix(
        blur_taps, offsets, wide_rows // DEC + 2 * low_reach, wide_rows + 2 * fine_reach
    )
    blurring = jnp.dot(lifting, lowering, precision=FULL_PRECISION)
    blurring = blurring[:, fine_reach : fine_reach + wide_rows]

    def operate(values):
        restored = apply_band(blurring, values)
        return (
            jnp.dot(restored, hyper_gram, precision=FULL_PRECISION)
            + jnp.dot(values, multi_gram, precision=FULL_PRECISION)
            + RIDGE_TERM * values
        )

    def own(values):
        return values[halo : halo + fine_rows]

    right_side = apply_band(lifting, hyper_wide) + multi_wide
    solution = start_wide
    residual = right_side - operate(solution)
    direction = residual
    norm_now = None
    for iteration in range(ITERS):
        mapped = operate(direction)
        parts = [
            jnp.sum(own(direction) * own(mapped)),
            jnp.sum(own(residual) * own(mapped)),
            jnp.sum(own(mapped) * own(mapped)),
        ]
        if norm_now is None:
            parts.append(jnp.sum(own(residual) * own(residual)))
            curvature, cross, power, norm_now = grid_totals(parts)
        else:
            curvature, cross, power = grid_totals(parts)
        step_size = norm_now / curvature
        solution = solution + step_size * direction
        residual = residual - step_size * mapped
        norm_next = norm_now - 2 * step_size * cross + step_size * step_size * power
        direction = residual + norm_next / norm_now * direction
        norm_now = norm_next
    solution = own(solution)
    residual = own(residual)
    return (solution, residual)


def solution(mesh):
    in_specs = (
        P(None, "row", "col"),
        P(None, "row", "col"),
        P(("row", "col"), None),
        P("col", "row"),
        P(),
        P(),
        P(),
        P(),
    )
    out_specs = (P(("row", "col"), None), P(("row", "col"), None))
    return jax.shard_map(body, mesh=mesh, in_specs=in_specs, out_specs=out_specs, check_vma=False)
```
